256 devices in a mesh: orb: 64 (over x, z, core), grp: 4 (over y).
Axes of the slice: x: 4, y: 4, z: 8, core: 2. Of those that a mesh axis runs over, the one named last changes fastest.
Arguments:
- orbitals: float32 [512, 48, 2304], P(('orb', 'grp')), may hold values from -6 to 6
- kernel: float32 [48, 2304], replicated, may hold values from 0.1 to 2
- anchors: int32 [64, 3], replicated, may hold values from 0 to 16
- pair_count: int32 [64], P('orb'), may hold values from 1 to 8, 256 in all
- pair_first: int32 [512], P('orb'), may hold values from 0 to 7
- pair_second: int32 [512], P('orb'), may hold values from 0 to 7
- pair_reach: int32 [512], P('orb'), may hold values from 0 to 2
Outputs:
- gradient: float32 [512, 48, 2304], P('orb', 'grp')
- lagrange: float32 [64, 8, 8], P('orb')
The draws below stay inside these ranges and needn't reach their ends.
Inputs may be any that keep to these rules, and one draw needn't show every extreme that they name: The live slots of a fragment are its first pair_count slots; some fragment has all 8 live.
All inputs are finite; a program needn't handle non-finite values. No bound on the sum of `pair_count` on one device may be relied on, other than what follows from the above.
Results may differ from the reference program's by a relative error of at most 0.0003.
Values sent between devices are 32-bit elements; how exact they have to be, the bound alone decides.
A program may use at most 128 MiB of HBM per device.

```python
import math
import jax
import jax.numpy as jnp
import numpy as np
from jax import lax

B = 48
ORB_DEV = 2
PF = 8
REACH = 2
FRAG_ORB = 8
ORB = 512
SHIFT_MAX = 16
N_ORB = 64
N_GRP = 4


def touch_ends(drawn, stream_key, smallest, high):
    index_at = [jax.random.randint(jax.random.fold_in(stream_key, axis), (), 0, length) for axis, length in enumerate(drawn.shape)]
    longest = drawn.shape.index(max(drawn.shape))
    next_to = index_at[:longest] + [(index_at[longest] + 1) % drawn.shape[longest]] + index_at[longest + 1:]
    return drawn.at[tuple(index_at)].set(smallest).at[tuple(next_to)].set(high)


def block_scale(rng, extent, pieces, least, high):
    gain, own = 1.0, jax.random.fold_in(rng, 6)
    for position, parts in pieces:
        heights = jnp.exp(jax.random.uniform(jax.random.fold_in(own, position), (parts,), jnp.float32, least / len(pieces), high / len(pieces)))
        gain = gain * jnp.repeat(heights, extent[position] // parts).reshape([-1 if axis == position else 1 for axis in range(len(extent))])
    return gain


def length_profile(amount, total, most, skew):
    portions = [(1 << 20) // math.isqrt(standing ** skew) + 1 for standing in range(2, amount + 1)]
    spare, counts = total - most - (amount - 1), [1] * (amount - 1)
    while spare > 0:
        free = [i for i in range(amount - 1) if counts[i] < most]
        pool, left = sum([portions[i] for i in free]), spare
        for i in free:
            extra = min(most - counts[i], max(1, left * portions[i] // pool), spare)
            counts[i] = counts[i] + extra
            spare = spare - extra
    return np.array([most] + counts)


def ragged(own_key, count, total, bound, skew):
    if count == 2:
        one = jax.random.randint(own_key, (), max(1, total - bound), min(bound, total - 1) + 1)
        return jnp.stack([one, total - one])
    sizes = jnp.asarray(length_profile(count, total, bound, skew), jnp.int32)
    couples = (count - 1) // 2
    giver, receiver = sizes[1:1 + 2 * couples:2], sizes[2:2 + 2 * couples:2]
    slack = jnp.minimum(giver - 1, bound - receiver)
    shifted = jax.random.randint(jax.random.fold_in(own_key, 1), (couples,), 0, 1 << 20) % (slack + 1)
    sizes = sizes.at[1:1 + 2 * couples:2].set(giver - shifted).at[2:2 + 2 * couples:2].set(receiver + shifted)
    return sizes[jax.random.permutation(jax.random.fold_in(own_key, 2), count)]


def normal_values(rng, extent, deviation, most, shards=(), kind=jnp.bfloat16):
    entries = deviation * jax.random.normal(rng, extent, jnp.float32)
    if shards:
        entries = entries * block_scale(rng, extent, shards, -0.22, 0.18)
    return jnp.clip(entries, -most, most).astype(kind)


def setup_inputs(seed: int = 0) -> dict:
    arg_keys = jax.random.split(jax.random.key(seed), 8)
    orbitals = normal_values(arg_keys[0], (ORB, B, B * B), 1.0, 6.0, ((0, 256),), jnp.float32)
    kernel = jnp.clip(jnp.exp(jax.random.uniform(arg_keys[1], (B, B * B), jnp.float32, math.log(0.1), math.log(2.0))), 0.1, 2.0)
    anchors = touch_ends(jax.random.randint(arg_keys[2], (N_ORB, 3), 0, SHIFT_MAX + 1), jax.random.fold_in(arg_keys[2], 1), 0, SHIFT_MAX).astype(jnp.int32)
    pair_count = ragged(arg_keys[3], N_ORB, N_ORB * PF // 2, PF, 2).astype(jnp.int32)
    pair_first = touch_ends(jax.random.randint(arg_keys[4], (N_ORB * PF,), 0, FRAG_ORB), jax.random.fold_in(arg_keys[4], 1), 0, FRAG_ORB - 1).astype(jnp.int32)
    pair_second = touch_ends(jax.random.randint(arg_keys[5], (N_ORB * PF,), 0, FRAG_ORB), jax.random.fold_in(arg_keys[5], 1), 0, FRAG_ORB - 1).astype(jnp.int32)
    pair_reach = touch_ends(jax.random.randint(arg_keys[6], (N_ORB * PF,), 0, REACH + 1), jax.random.fold_in(arg_keys[6], 1), 0, REACH).astype(jnp.int32)
    return dict(orbitals=orbitals, kernel=kernel, anchors=anchors, pair_count=pair_count, pair_first=pair_first, pair_second=pair_second, pair_reach=pair_reach)


def offset_matrix(offset, count):
    rows = jnp.arange(count, dtype=jnp.int32)
    return (rows[None, :] == rows[:, None] - offset).astype(jnp.float32)


def cycle(matrices, volume):
    box_edge = volume.shape[0]
    for matrix in matrices:
        product = jnp.dot(matrix, volume, precision=lax.Precision.HIGHEST, preferred_element_type=jnp.float32)
        volume = product.reshape(box_edge, box_edge, box_edge).transpose(1, 2, 0).reshape(box_edge, box_edge * box_edge)
    return volume


def reference(orbitals, kernel, anchors, pair_count, pair_first, pair_second, pair_reach):
    frag_size = ORB_DEV * N_GRP
    cube = kernel.reshape(B, B, B)

    def solve(accum, slot):
        fragment = slot // PF
        within = slot % PF
        first = pair_first[slot]
        second = pair_second[slot]
        reach = pair_reach[slot]
        partner = (fragment + reach) % N_ORB
        index_first = (fragment * frag_size + first).astype(jnp.int32)
        index_second = (partner * frag_size + second).astype(jnp.int32)
        delta = anchors[partner] - anchors[fragment]
        matrices = [offset_matrix(delta[0], B), offset_matrix(delta[1], B), offset_matrix(delta[2], B)]
        phi_first = orbitals[index_first]
        phi_second = orbitals[index_second]
        moved = cycle(matrices, phi_second)
        density = phi_first * moved
        spectrum = jnp.fft.fftn(density.reshape(B, B, B))
        potential = jnp.real(jnp.fft.ifftn(cube * spectrum)).astype(jnp.float32).reshape(B, B * B)
        weight = (within < pair_count[fragment]).astype(jnp.float32)
        accum = accum.at[index_first].add(weight * potential * moved)
        back = cycle([matrix.T for matrix in matrices], potential * phi_first)
        accum = accum.at[index_second].add(weight * back)
        return accum, None

    start = jnp.zeros(orbitals.shape, jnp.float32)
    action, _ = lax.scan(solve, start, jnp.arange(N_ORB * PF, dtype=jnp.int32))
    phi = orbitals.reshape(N_ORB, frag_size, B * B * B)
    acted = action.reshape(N_ORB, frag_size, B * B * B)
    correlation = jnp.einsum('fan,fbn->fab', phi, acted, precision=lax.Precision.HIGHEST) / (B ** 3)
    lagrange = 0.5 * (correlation + jnp.swapaxes(correlation, 1, 2))
    gradient = acted - jnp.einsum('fba,fbn->fan', lagrange, phi, precision=lax.Precision.HIGHEST)
    return gradient.reshape(orbitals.shape), lagrange
```

```python
import functools
import math

import jax
import jax.numpy as jnp
import ml_dtypes
import numpy as np
from jax import lax
from jax.experimental import pallas as pl
from jax.experimental.pallas import tpu as pltpu
from jax.sharding import PartitionSpec as P

MESH = pl.DeviceIdType.MESH
B = 48
FRAG = 8
GRP = 4
TURNS = 2
TILES = 18
SLAB = 216
ROWS = 864
HALF = 25
CH = 152
PADX = 16
PADT = 8


def split(a):
    a = a.astype(np.float32)
    head = a.astype(ml_dtypes.bfloat16)
    tail = (a - head.astype(np.float32)).astype(ml_dtypes.bfloat16)
    return head, tail


@functools.lru_cache(None)
def tables():
    c, kx = np.meshgrid(np.arange(6), np.arange(HALF), indexing="ij")
    c, kx = c.reshape(-1, 1), kx.reshape(-1, 1)
    a, x = np.meshgrid(np.arange(6), np.arange(B), indexing="ij")
    a, x = a.reshape(1, -1), x.reshape(1, -1)
    theta = 2 * np.pi * ((8 * c * a + kx * x) % 48) / 48
    left = np.zeros((2 * CH, 288))
    left[:150] = np.cos(theta)
    left[CH:CH + 150] = -np.sin(theta)
    head, tail = split(left)
    fwd_left = np.concatenate([head, head, tail], axis=1)
    inv_left = np.concatenate([head.T, head.T, tail.T], axis=1)
    b, z = np.meshgrid(np.arange(8), np.arange(B), indexing="ij")
    b, z = b.reshape(-1), z.reshape(-1)
    phi = 2 * np.pi * ((6 * np.outer(b, b) + np.outer(z, z)) % 48) / 48
    head, tail = split(np.concatenate([np.cos(phi), -np.sin(phi)], axis=1))
    right = np.concatenate([head, head, tail], axis=0)
    turn = 2 * np.pi * ((c * b[None, :]) % 48) / 48
    twiddle = np.zeros((2, CH, 384), np.float32)
    twiddle[0, :150] = np.cos(turn)
    twiddle[1, :150] = -np.sin(turn)
    return fwd_left, inv_left, right, twiddle


def mode_table(kernel):
    cube = kernel.reshape(B, B, B)
    flipped = jnp.roll(jnp.flip(cube, (0, 1, 2)), (1, 1, 1), (0, 1, 2))
    even = (cube[:HALF] + flipped[:HALF]) * 0.5
    weight = np.full((HALF, 1, 1), 2.0 / B**3, np.float32)
    weight[0] = weight[HALF - 1] = 1.0 / B**3
    even = (even * weight).reshape(HALF, 8, 6, B).transpose(2, 0, 1, 3).reshape(6 * HALF, 384)
    return jnp.pad(even, ((0, CH - 6 * HALF), (0, 0)))


def halves(value):
    head = value.astype(jnp.bfloat16)
    return head, (value - head.astype(jnp.float32)).astype(jnp.bfloat16)


def dot(a, b):
    return jnp.dot(a, b, preferred_element_type=jnp.float32)


def shifted(source, offset, emit):
    d0, d1, d2 = offset
    flat = 48 * d1 + d2 + 1024
    tile = lax.shift_right_logical(flat, 7) - 8
    lane_by = lax.bitwise_and(flat, 127)
    lane = lax.broadcasted_iota(jnp.int32, (B, 128), 1)
    late = lane >= lane_by
    insides = []
    for k in range(3):
        z = lax.rem(lane + 128 * k, B) - d2
        insides.append((z >= 0) & (z < B))
    before = None
    for t in range(-1, TILES):
        block = source[t - tile + PADT, pl.ds(PADX - d0, B), :]
        block = pltpu.roll(block, lane_by, 1)
        if t >= 0:
            emit(t, jnp.where(insides[t % 3], jnp.where(late, block, before), 0.0))
        before = block


def pair_kernel(first_ref, second_ref, modes_ref, fwd_left, inv_left, right, twiddle,
                anchors, reach_ref, out_ref, padded, boxes, moved, stack, wide, spec, volume):
    frag, member = lax.axis_index("orb"), lax.axis_index("grp")

    def offset_of(turn):
        partner = lax.rem(frag + reach_ref[member + GRP * turn], lax.axis_size("orb"))
        return [anchors[partner, k] - anchors[frag, k] for k in range(3)]

    padded[...] = jnp.zeros_like(padded)

    def at(t):
        return slice(48 * (t // 3), 48 * (t // 3) + 48), slice(128 * (t % 3), 128 * (t % 3) + 128)

    for turn in range(TURNS):
        for s in range(GRP):
            boxes[0, pl.ds(SLAB * s, SLAB), :] = first_ref[s, turn]
            boxes[1, pl.ds(SLAB * s, SLAB), :] = second_ref[s, turn]
        for t in range(TILES):
            padded[t + PADT, pl.ds(PADX, B), :] = boxes[1, pl.ds(t, B, stride=TILES), :]

        def emit(t, block):
            moved[turn, t] = block
            density = boxes[0, pl.ds(t, B, stride=TILES), :] * block
            head, tail = halves(density)
            rows, lanes = at(t)
            lanes = slice(384 * turn + lanes.start, 384 * turn + lanes.stop)
            stack[rows.start:rows.stop, lanes] = head
            stack[288 + rows.start:288 + rows.stop, lanes] = tail
            stack[576 + rows.start:576 + rows.stop, lanes] = head

        shifted(padded, offset_of(turn), emit)

    volume[0:2 * CH, :] = dot(fwd_left[...], stack[0:864, :])
    tr, ti = twiddle[0], twiddle[1]

    def put(row, value):
        head, tail = halves(value)
        wide[row:row + CH, 0:384] = head
        wide[row:row + CH, 384:768] = tail
        wide[row:row + CH, 768:1152] = head

    for turn in range(TURNS):
        re = volume[0:CH, 384 * turn:384 * turn + 384]
        im = volume[CH:2 * CH, 384 * turn:384 * turn + 384]
        put(2 * CH * turn, re * tr - im * ti)
        put(2 * CH * turn + CH, re * ti + im * tr)
    spec[...] = dot(wide[...], right[...])
    table = modes_ref[...]
    for turn in range(TURNS):
        row = 2 * CH * turn
        re = spec[row:row + CH, 0:384] - spec[row + CH:row + 2 * CH, 384:768]
        im = spec[row:row + CH, 384:768] + spec[row + CH:row + 2 * CH, 0:384]
        put(row, re * table)
        put(row + CH, im * table)
    spec[...] = dot(wide[...], right[...])
    for turn in range(TURNS):
        row = 2 * CH * turn
        re = spec[row:row + CH, 0:384] + spec[row + CH:row + 2 * CH, 384:768]
        im = spec[row + CH:row + 2 * CH, 0:384] - spec[row:row + CH, 384:768]
        lanes = slice(384 * turn, 384 * turn + 384)
        for part, value in enumerate((re * tr + im * ti, im * tr - re * ti)):
            head, tail = halves(value)
            stack[CH * part:CH * part + CH, lanes] = head
            stack[304 + CH * part:304 + CH * part + CH, lanes] = tail
            stack[608 + CH * part:608 + CH * part + CH, lanes] = head
    volume[0:288, :] = dot(inv_left[...], stack[...])

    for turn in range(TURNS):
        for s in range(GRP):
            boxes[0, pl.ds(SLAB * s, SLAB), :] = first_ref[s, turn]
        for t in range(TILES):
            rows, lanes = at(t)
            potential = volume[rows, 384 * turn + lanes.start:384 * turn + lanes.stop]
            out_ref[turn, 0, pl.ds(t, B, stride=TILES), :] = potential * moved[turn, t]
            padded[t + PADT, pl.ds(PADX, B), :] = potential * boxes[0, pl.ds(t, B, stride=TILES), :]

        def emit(t, block):
            out_ref[turn, 1, pl.ds(t, B, stride=TILES), :] = block

        shifted(padded, [-d for d in offset_of(turn)], emit)


def pair_terms(first, second, modes, anchors, reach):
    fwd_left, inv_left, right, twiddle = tables()
    vmem, smem = pl.BlockSpec(memory_space=pltpu.VMEM), pl.BlockSpec(memory_space=pltpu.SMEM)
    return pl.pallas_call(
        pair_kernel,
        out_shape=jax.ShapeDtypeStruct((TURNS, 2, ROWS, 128), jnp.float32),
        in_specs=[vmem] * 7 + [smem] * 2,
        out_specs=vmem,
        scratch_shapes=[
            pltpu.VMEM((TILES + 2 * PADT, B + 2 * PADX, 128), jnp.float32),
            pltpu.VMEM((2, ROWS, 128), jnp.float32),
            pltpu.VMEM((TURNS, TILES, B, 128), jnp.float32),
            pltpu.VMEM((912, 768), jnp.bfloat16),
            pltpu.VMEM((2 * TURNS * CH, 1152), jnp.bfloat16),
            pltpu.VMEM((2 * TURNS * CH, 768), jnp.float32),
            pltpu.VMEM((2 * CH, 768), jnp.float32),
        ],
        compiler_params=pltpu.CompilerParams(vmem_limit_bytes=60 << 20),
        name="pair_terms",
    )(first, second, modes, jnp.asarray(fwd_left), jnp.asarray(inv_left), jnp.asarray(right),
      jnp.asarray(twiddle), anchors, reach)


def gather_kernel(terms_ref, count, first, second, reach, acc_ref):
    acc_ref[...] = jnp.zeros_like(acc_ref)
    for slot in range(GRP * TURNS):
        @pl.when(slot < count[0])
        def _():
            turn, member = slot // GRP, slot % GRP
            acc_ref[0, first[slot]] += terms_ref[turn, 0, member]
            acc_ref[reach[slot], second[slot]] += terms_ref[turn, 1, member]


def gathered(terms, count, first, second, reach):
    vmem, smem = pl.BlockSpec(memory_space=pltpu.VMEM), pl.BlockSpec(memory_space=pltpu.SMEM)
    return pl.pallas_call(
        gather_kernel,
        out_shape=jax.ShapeDtypeStruct((3, FRAG, SLAB, 128), jnp.float32),
        in_specs=[vmem] + [smem] * 4,
        out_specs=vmem,
        compiler_params=pltpu.CompilerParams(vmem_limit_bytes=40 << 20),
        name="gathered",
    )(terms, count, first, second, reach)


def correlate_kernel(phi_ref, own_ref, one_ref, two_ref, action_ref, total_ref, block, landed, send_sem, recv_sem):
    me = lax.axis_index("grp")
    barrier = pltpu.get_barrier_semaphore()
    for step in range(1, GRP):
        pl.semaphore_signal(barrier, inc=1, device_id={"grp": lax.rem(me + step, GRP)}, device_id_type=MESH)
    row = lax.broadcasted_iota(jnp.int32, (FRAG, 128), 0)
    lane = lax.broadcasted_iota(jnp.int32, (FRAG, 128), 1)
    for b in range(FRAG):
        action_ref[b] = own_ref[b] + one_ref[b] + two_ref[b]
    total = jnp.zeros((FRAG, 128), jnp.float32)
    for b in range(FRAG):
        act = action_ref[b]
        for a in range(FRAG):
            part = jnp.sum(phi_ref[a] * act, axis=0, keepdims=True)
            part = jnp.sum(part, axis=1, keepdims=True)
            total = total + jnp.where((row == a) & (lane == b), part, 0.0)
    block[...] = total
    pl.semaphore_wait(barrier, GRP - 1)
    copies = []
    for step in range(1, GRP):
        copies.append(pltpu.make_async_remote_copy(
            src_ref=block, dst_ref=landed.at[step], send_sem=send_sem.at[step], recv_sem=recv_sem.at[step],
            device_id={"grp": lax.rem(me + step, GRP)}, device_id_type=MESH))
    for copy in copies:
        copy.start()
    for copy in copies:
        copy.wait()
    total_ref[...] = ((block[...] + landed[2]) + (landed[1] + landed[3])) / float(B**3)


def correlated(phi, own, one, two):
    vmem = pl.BlockSpec(memory_space=pltpu.VMEM)
    return pl.pallas_call(
        correlate_kernel,
        out_shape=(jax.ShapeDtypeStruct((FRAG, SLAB, 128), jnp.float32),
                   jax.ShapeDtypeStruct((FRAG, 128), jnp.float32)),
        in_specs=[vmem] * 4,
        out_specs=(vmem, vmem),
        scratch_shapes=[
            pltpu.VMEM((FRAG, 128), jnp.float32),
            pltpu.VMEM((GRP, FRAG, 128), jnp.float32),
            pltpu.SemaphoreType.DMA((GRP,)),
            pltpu.SemaphoreType.DMA((GRP,)),
        ],
        compiler_params=pltpu.CompilerParams(
            collective_id=0, has_side_effects=True, vmem_limit_bytes=40 << 20),
        name="correlated",
    )(phi, own, one, two)


def project_kernel(phi_ref, action_ref, total_ref, gradient_ref, lagrange_ref):
    total = total_ref[...][:, 0:FRAG]
    lagrange = 0.5 * (total + total.T)
    lagrange_ref[0] = lagrange
    for a in range(FRAG):
        for t in range(TILES):
            value = action_ref[a, pl.ds(t, 12, stride=TILES), :]
            for b in range(FRAG):
                value = value - lagrange[b:b + 1, a:a + 1] * phi_ref[b, pl.ds(t, 12, stride=TILES), :]
            gradient_ref[a, :, 128 * t:128 * t + 128] = value


def projected(phi, action, total):
    vmem = pl.BlockSpec(memory_space=pltpu.VMEM)
    return pl.pallas_call(
        project_kernel,
        out_shape=(jax.ShapeDtypeStruct((FRAG, 12, B * B), jnp.float32),
                   jax.ShapeDtypeStruct((1, FRAG, FRAG), jnp.float32)),
        in_specs=[vmem] * 3,
        out_specs=(vmem, vmem),
        compiler_params=pltpu.CompilerParams(vmem_limit_bytes=40 << 20),
        name="projected",
    )(phi, action, total)


def passed_along(block, distance):
    count = lax.axis_size("orb")
    return lax.ppermute(block, "orb", [((i - distance) % count, i) for i in range(count)])


def shards(orbitals, kernel, anchors, pair_count, pair_first, pair_second, pair_reach):
    phi = lax.all_to_all(orbitals.reshape(2, GRP, SLAB, 128), "grp", split_axis=1, concat_axis=0, tiled=True)
    phi = phi.reshape(FRAG, SLAB, 128)
    ahead = [passed_along(phi, -r) for r in (1, 2)]
    modes = mode_table(kernel)
    nearby = jnp.stack([phi] + ahead)
    order = np.arange(GRP * TURNS).reshape(TURNS, GRP).T.reshape(-1)
    first = phi[pair_first[order]].reshape(GRP, TURNS, SLAB, 128)
    second = nearby[pair_reach[order], pair_second[order]].reshape(GRP, TURNS, SLAB, 128)
    first = lax.all_to_all(first, "grp", split_axis=0, concat_axis=0, tiled=True)
    second = lax.all_to_all(second, "grp", split_axis=0, concat_axis=0, tiled=True)
    terms = pair_terms(first, second, modes, anchors, pair_reach)
    terms = terms.reshape(TURNS, 2, GRP, SLAB, 128)
    terms = lax.all_to_all(terms, "grp", split_axis=2, concat_axis=2, tiled=True)
    acc = gathered(terms, pair_count, pair_first, pair_second, pair_reach)
    one, two = (passed_along(acc[r], r) for r in (1, 2))
    action, total = correlated(phi, acc[0], one, two)
    return projected(phi, action, total)


def solution(mesh):
    placed = (P(("orb", "grp"), None, None), P(), P(), P("orb"), P("orb"), P("orb"), P("orb"))
    return jax.shard_map(
        shards,
        mesh=mesh,
        in_specs=placed,
        out_specs=(P("orb", "grp", None), P("orb", None, None)),
        check_vma=False,
    )
```

```python
import functools
import math

import jax
import jax.numpy as jnp
import ml_dtypes
import numpy as np
from jax import lax
from jax.experimental import pallas as pl
from jax.experimental.pallas import tpu as pltpu
from jax.sharding import PartitionSpec as P

MESH = pl.DeviceIdType.MESH
B = 48
FRAG = 8
GRP = 4
TURNS = 2
TILES = 18
SLAB = 216
ROWS = 864
HALF = 25
CH = 152
PADX = 16
PADT = 8
CHUNKS = 3
CHUNK = SLAB // CHUNKS


def split(a):
    a = a.astype(np.float32)
    head = a.astype(ml_dtypes.bfloat16)
    tail = (a - head.astype(np.float32)).astype(ml_dtypes.bfloat16)
    return head, tail


@functools.lru_cache(None)
def tables():
    c, kx = np.meshgrid(np.arange(6), np.arange(HALF), indexing="ij")
    c, kx = c.reshape(-1, 1), kx.reshape(-1, 1)
    a, x = np.meshgrid(np.arange(6), np.arange(B), indexing="ij")
    a, x = a.reshape(1, -1), x.reshape(1, -1)
    theta = 2 * np.pi * ((8 * c * a + kx * x) % 48) / 48
    left = np.zeros((2 * CH, 288))
    left[:150] = np.cos(theta)
    left[CH:CH + 150] = -np.sin(theta)
    left = np.concatenate(split(left), axis=1)
    inverse = np.concatenate([left[:, :288].T, left[:, 288:].T], axis=1)
    b, z = np.meshgrid(np.arange(8), np.arange(B), indexing="ij")
    b, z = b.reshape(-1), z.reshape(-1)
    phi = 2 * np.pi * ((6 * np.outer(b, b) + np.outer(z, z)) % 48) / 48
    right = np.concatenate(split(np.concatenate([np.cos(phi), -np.sin(phi)], axis=1)), axis=0)
    turn = 2 * np.pi * ((np.arange(6)[:, None] * b[None, :]) % 48) / 48
    twiddle = np.stack([np.cos(turn), -np.sin(turn)]).astype(np.float32)
    return left, inverse, right, twiddle


def halves(value):
    head = value.astype(jnp.bfloat16)
    return head, (value - head.astype(jnp.float32)).astype(jnp.bfloat16)


def dot(a, b):
    return jnp.dot(a, b, preferred_element_type=jnp.float32)


def modes_kernel(kernel_ref, modes_ref, picked, mirrored):
    for c in range(6):
        for e in range(8):
            picked[48 * c:48 * c + 48, 48 * e:48 * e + 48] = kernel_ref[:, 48 * (c + 6 * e):48 * (c + 6 * e) + 48]
    lane = lax.broadcasted_iota(jnp.int32, (1, 384), 1)
    e, kz = lane // B, lane % B
    row = lax.broadcasted_iota(jnp.int32, (384, 384), 0)
    for shift, rows in ((0, slice(0, 48)), (1, slice(48, 288))):
        source = (16 - e - shift) % 8 * B + (B - kz) % B
        permute = jnp.where(row == source, 1.0, 0.0).astype(jnp.bfloat16)
        head, tail = halves(picked[rows, :])
        mirrored[rows, :] = dot(head, permute) + dot(tail, permute)
    out = lax.broadcasted_iota(jnp.int32, (32, B), 0)
    permute = jnp.where(lax.broadcasted_iota(jnp.int32, (32, B), 1) == (B - out) % B, 1.0, 0.0).astype(jnp.bfloat16)
    kx = lax.broadcasted_iota(jnp.int32, (32, 384), 0)
    weight = jnp.where((kx == 0) | (kx == HALF - 1), 0.5 / B**3, 1.0 / B**3)
    modes_ref[144:CH, :] = jnp.zeros((8, 384), jnp.float32)
    for c in range(6):
        other = (6 - c) % 6
        head, tail = halves(mirrored[48 * other:48 * other + 48, :])
        even = (picked[48 * c:48 * c + 32, :] + dot(permute, head) + dot(permute, tail)) * weight
        modes_ref[HALF * c:HALF * c + HALF, :] = even[:HALF]


def mode_table(kernel):
    vmem = pl.BlockSpec(memory_space=pltpu.VMEM)
    return pl.pallas_call(
        modes_kernel,
        out_shape=jax.ShapeDtypeStruct((CH, 384), jnp.float32),
        in_specs=[vmem],
        out_specs=vmem,
        scratch_shapes=[pltpu.VMEM((288, 384), jnp.float32), pltpu.VMEM((288, 384), jnp.float32)],
        compiler_params=pltpu.CompilerParams(vmem_limit_bytes=40 << 20),
        name="mode_table",
    )(kernel)


def shifted(source, offset, emit):
    d0, d1, d2 = offset
    flat = 48 * d1 + d2 + 1024
    tile = lax.shift_right_logical(flat, 7) - 8
    lane_by = lax.bitwise_and(flat, 127)
    lane = lax.broadcasted_iota(jnp.int32, (B, 128), 1)
    late = lane >= lane_by
    insides = []
    for k in range(3):
        z = lax.rem(lane + 128 * k, B) - d2
        insides.append((z >= 0) & (z < B))
    before = None
    for t in range(-1, TILES):
        block = source[t - tile + PADT, pl.ds(PADX - d0, B), :]
        block = pltpu.roll(block, lane_by, 1)
        if t >= 0:
            emit(t, jnp.where(insides[t % 3], jnp.where(late, block, before), 0.0))
        before = block


def pair_kernel(pairs_ref, modes_ref, left_ref, inverse_ref, right_ref, twiddle_ref, anchors, reach_ref,
                out_ref, padded, moved, stack, wide, spec, volume, left, inverse, right, twiddle):
    left[:, 0:288] = left_ref[:, 0:288]
    left[:, 288:864] = left_ref[...]
    inverse[:, 0:304] = inverse_ref[:, 0:304]
    inverse[:, 304:912] = inverse_ref[...]
    right[0:384, :] = right_ref[0:384, :]
    right[384:1152, :] = right_ref[...]
    for c in range(6):
        rows = slice(HALF * c, HALF * c + HALF + 2 * (c == 5))
        for part in range(2):
            twiddle[part, rows, :] = jnp.broadcast_to(twiddle_ref[part, c:c + 1, :], (rows.stop - rows.start, 384))
    frag, member = lax.axis_index("orb"), lax.axis_index("grp")

    def offset_of(turn):
        partner = lax.rem(frag + reach_ref[member + GRP * turn], lax.axis_size("orb"))
        return [anchors[partner, k] - anchors[frag, k] for k in range(3)]

    padded[...] = jnp.zeros_like(padded)

    def at(t):
        return slice(48 * (t // 3), 48 * (t // 3) + 48), slice(128 * (t % 3), 128 * (t % 3) + 128)

    for turn in range(TURNS):
        for t in range(TILES):
            padded[t + PADT, pl.ds(PADX, B), :] = pairs_ref[turn, 1, pl.ds(t, B, stride=TILES), :]

        def emit(t, block):
            moved[turn, t] = block
            density = pairs_ref[turn, 0, pl.ds(t, B, stride=TILES), :] * block
            head, tail = halves(density)
            rows, lanes = at(t)
            lanes = slice(384 * turn + lanes.start, 384 * turn + lanes.stop)
            stack[rows.start:rows.stop, lanes] = head
            stack[288 + rows.start:288 + rows.stop, lanes] = tail
            stack[576 + rows.start:576 + rows.stop, lanes] = head

        shifted(padded, offset_of(turn), emit)

    volume[0:2 * CH, :] = dot(left[...], stack[0:864, :])
    tr, ti = twiddle[0], twiddle[1]

    def put(row, value):
        head, tail = halves(value)
        wide[row:row + CH, 0:384] = head
        wide[row:row + CH, 384:768] = tail
        wide[row:row + CH, 768:1152] = head

    for turn in range(TURNS):
        re = volume[0:CH, 384 * turn:384 * turn + 384]
        im = volume[CH:2 * CH, 384 * turn:384 * turn + 384]
        put(2 * CH * turn, re * tr - im * ti)
        put(2 * CH * turn + CH, re * ti + im * tr)
    spec[...] = dot(wide[...], right[...])
    table = modes_ref[...]
    for turn in range(TURNS):
        row = 2 * CH * turn
        re = spec[row:row + CH, 0:384] - spec[row + CH:row + 2 * CH, 384:768]
        im = spec[row:row + CH, 384:768] + spec[row + CH:row + 2 * CH, 0:384]
        put(row, re * table)
        put(row + CH, im * table)
    spec[...] = dot(wide[...], right[...])
    for turn in range(TURNS):
        row = 2 * CH * turn
        re = spec[row:row + CH, 0:384] + spec[row + CH:row + 2 * CH, 384:768]
        im = spec[row + CH:row + 2 * CH, 0:384] - spec[row:row + CH, 384:768]
        lanes = slice(384 * turn, 384 * turn + 384)
        for part, value in enumerate((re * tr + im * ti, im * tr - re * ti)):
            head, tail = halves(value)
            stack[CH * part:CH * part + CH, lanes] = head
            stack[304 + CH * part:304 + CH * part + CH, lanes] = tail
            stack[608 + CH * part:608 + CH * part + CH, lanes] = head
    volume[0:288, :] = dot(inverse[...], stack[...])

    for turn in range(TURNS):
        for t in range(TILES):
            rows, lanes = at(t)
            potential = volume[rows, 384 * turn + lanes.start:384 * turn + lanes.stop]
            out_ref[turn, 0, pl.ds(t, B, stride=TILES), :] = potential * moved[turn, t]
            padded[t + PADT, pl.ds(PADX, B), :] = potential * pairs_ref[turn, 0, pl.ds(t, B, stride=TILES), :]

        def emit(t, block):
            out_ref[turn, 1, pl.ds(t, B, stride=TILES), :] = block

        shifted(padded, [-d for d in offset_of(turn)], emit)


def pair_terms(pairs, modes, anchors, reach):
    left, inverse, right, twiddle = tables()
    vmem, smem = pl.BlockSpec(memory_space=pltpu.VMEM), pl.BlockSpec(memory_space=pltpu.SMEM)
    return pl.pallas_call(
        pair_kernel,
        out_shape=jax.ShapeDtypeStruct((TURNS, 2, ROWS, 128), jnp.float32),
        in_specs=[vmem] * 6 + [smem] * 2,
        out_specs=vmem,
        scratch_shapes=[
            pltpu.VMEM((TILES + 2 * PADT, B + 2 * PADX, 128), jnp.float32),
            pltpu.VMEM((TURNS, TILES, B, 128), jnp.float32),
            pltpu.VMEM((912, 768), jnp.bfloat16),
            pltpu.VMEM((2 * TURNS * CH, 1152), jnp.bfloat16),
            pltpu.VMEM((2 * TURNS * CH, 768), jnp.float32),
            pltpu.VMEM((2 * CH, 768), jnp.float32),
            pltpu.VMEM((2 * CH, 864), jnp.bfloat16),
            pltpu.VMEM((288, 912), jnp.bfloat16),
            pltpu.VMEM((1152, 768), jnp.bfloat16),
            pltpu.VMEM((2, CH, 384), jnp.float32),
        ],
        compiler_params=pltpu.CompilerParams(vmem_limit_bytes=56 << 20),
        name="pair_terms",
    )(pairs, modes, jnp.asarray(left), jnp.asarray(inverse), jnp.asarray(right), jnp.asarray(twiddle), anchors, reach)


def sibling(orb):
    return orb + 1 - 2 * lax.rem(orb, 2)


def greet(orb, member):
    barrier = pltpu.get_barrier_semaphore()
    orbs = lax.axis_size("orb")
    for step in range(1, GRP):
        pl.semaphore_signal(barrier, inc=1, device_id={"grp": lax.rem(member + step, GRP)}, device_id_type=MESH)
    for other in (sibling(orb), lax.rem(orb + 2, orbs), lax.rem(orb + orbs - 2, orbs)):
        pl.semaphore_signal(barrier, inc=1, device_id={"orb": other}, device_id_type=MESH)
    pl.semaphore_wait(barrier, GRP - 1 + 3)


def spread_kernel(mine, first, second, reach, phi_ref, pairs_ref, *scratch):
    near = scratch[0:3 * CHUNKS]
    out = scratch[3 * CHUNKS:5 * CHUNKS]
    send_slab, recv_slab, own_sem, send_ahead, recv_ahead, send_side, recv_side, send_pick, recv_pick = scratch[5 * CHUNKS:]
    orb, me = lax.axis_index("orb"), lax.axis_index("grp")
    orbs = lax.axis_size("orb")
    even = lax.rem(orb, 2) == 0
    behind = lax.rem(orb + orbs - 2, orbs)
    greet(orb, me)

    def rows(c):
        return pl.ds(CHUNK * c, CHUNK)

    slabs, owns = [], []
    for c in range(CHUNKS):
        group = []
        for step in (2, 1, 3):
            other = lax.rem(me + step, GRP)
            group.append(pltpu.make_async_remote_copy(
                src_ref=mine.at[:, other, rows(c)], dst_ref=near[3 * c].at[pl.ds(2 * me, 2)],
                send_sem=send_slab.at[c, step], recv_sem=recv_slab.at[c, step],
                device_id={"grp": other}, device_id_type=MESH))
        slabs.append(group)
        owns.append(pltpu.make_async_copy(mine.at[:, me, rows(c)], near[3 * c].at[pl.ds(2 * me, 2)], own_sem.at[c]))
        owns[c].start()
        for copy in group:
            copy.start()

    ahead = [pltpu.make_async_remote_copy(
        src_ref=near[3 * c], dst_ref=near[3 * c + 2], send_sem=send_ahead.at[c], recv_sem=recv_ahead.at[c],
        device_id={"orb": behind}, device_id_type=MESH) for c in range(CHUNKS)]
    side = [[pltpu.make_async_remote_copy(
        src_ref=near[3 * c + which], dst_ref=near[3 * c + 1], send_sem=send_side.at[c], recv_sem=recv_side.at[c],
        device_id={"orb": sibling(orb)}, device_id_type=MESH) for which in (2, 0)] for c in range(CHUNKS)]

    def picks(which, c):
        copies = []
        for step in (2, 1, 3):
            other = lax.rem(me + step, GRP)
            copies.append(pltpu.make_async_remote_copy(
                src_ref=out[2 * c + which].at[other],
                dst_ref=pairs_ref.at[:, which, pl.ds(SLAB * me + CHUNK * c, CHUNK)],
                send_sem=send_pick.at[which, c, step], recv_sem=recv_pick.at[which, c, step],
                device_id={"grp": other}, device_id_type=MESH))
        return copies

    picked = [[picks(which, c) for c in range(CHUNKS)] for which in range(2)]

    def choose(which, c):
        for slot in range(GRP * TURNS):
            if which == 0:
                value = near[3 * c][first[slot]]
            else:
                value = near[3 * c][second[slot]]
                value = jnp.where(reach[slot] == 1, near[3 * c + 1][second[slot]], value)
                value = jnp.where(reach[slot] == 2, near[3 * c + 2][second[slot]], value)
            out[2 * c + which][slot % GRP, slot // GRP] = value
        for copy in picked[which][c]:
            copy.start()
        pairs_ref[:, which, pl.ds(pl.multiple_of(SLAB * me + CHUNK * c, 8), CHUNK), :] = out[2 * c + which][me]

    for c in range(CHUNKS):
        owns[c].wait()
        for copy in slabs[c]:
            copy.wait_recv()
        ahead[c].start()

        @pl.when(jnp.logical_not(even))
        def _():
            side[c][1].start()

        choose(0, c)
        phi_ref[:, CHUNK * c:CHUNK * c + CHUNK, :] = near[3 * c][...]
    for c in range(CHUNKS + 1):
        if c < CHUNKS:
            ahead[c].wait_recv()

            @pl.when(even)
            def _():
                side[c][0].start()

        if c > 0:
            side[c - 1][0].wait_recv()
            choose(1, c - 1)
    for c in range(CHUNKS):
        for copy in slabs[c]:
            copy.wait_send()
        ahead[c].wait_send()

        @pl.when(even)
        def _():
            side[c][0].wait_send()

        @pl.when(jnp.logical_not(even))
        def _():
            side[c][1].wait_send()

        for which in range(2):
            for copy in picked[which][c]:
                copy.wait()


def spread(mine, first, second, reach):
    vmem, smem = pl.BlockSpec(memory_space=pltpu.VMEM), pl.BlockSpec(memory_space=pltpu.SMEM)
    dma = pltpu.SemaphoreType.DMA
    return pl.pallas_call(
        spread_kernel,
        out_shape=(jax.ShapeDtypeStruct((FRAG, SLAB, 128), jnp.float32),
                   jax.ShapeDtypeStruct((TURNS, 2, ROWS, 128), jnp.float32)),
        in_specs=[vmem] + [smem] * 3,
        out_specs=(vmem, vmem),
        scratch_shapes=[pltpu.VMEM((FRAG, CHUNK, 128), jnp.float32)] * (3 * CHUNKS)
        + [pltpu.VMEM((GRP, TURNS, CHUNK, 128), jnp.float32)] * (2 * CHUNKS)
        + [dma((CHUNKS, GRP)), dma((CHUNKS, GRP)), dma((CHUNKS,)), dma((CHUNKS,)), dma((CHUNKS,)),
           dma((CHUNKS,)), dma((CHUNKS,)), dma((2, CHUNKS, GRP)), dma((2, CHUNKS, GRP))],
        compiler_params=pltpu.CompilerParams(collective_id=0, has_side_effects=True, vmem_limit_bytes=40 << 20),
        name="spread",
    )(mine, first, second, reach)


def collect_kernel(terms, phi_ref, count, first, second, reach, action_ref, total_ref, *scratch):
    landed = scratch[0:CHUNKS]
    aside = scratch[CHUNKS:2 * CHUNKS]
    beside = scratch[2 * CHUNKS:3 * CHUNKS]
    onward = scratch[3 * CHUNKS:4 * CHUNKS]
    behind = scratch[4 * CHUNKS:5 * CHUNKS]
    (products, block, blocks, send_term, recv_term, send_side, recv_side, send_on, recv_on,
     send_sum, recv_sum) = scratch[5 * CHUNKS:]
    orb, me = lax.axis_index("orb"), lax.axis_index("grp")
    orbs = lax.axis_size("orb")
    even = jnp.where(lax.rem(orb, 2) == 0, 1.0, 0.0)
    greet(orb, me)

    def rows(c):
        return pl.ds(CHUNK * c, CHUNK)

    moved = []
    for c in range(CHUNKS):
        group = []
        for step in (2, 1, 3):
            other = lax.rem(me + step, GRP)
            group.append(pltpu.make_async_remote_copy(
                src_ref=terms.at[:, :, other, rows(c)], dst_ref=landed[c].at[me],
                send_sem=send_term.at[c, step], recv_sem=recv_term.at[c, step],
                device_id={"grp": other}, device_id_type=MESH))
        moved.append(group)
        for copy in group:
            copy.start()
    side = [pltpu.make_async_remote_copy(
        src_ref=aside[c], dst_ref=beside[c], send_sem=send_side.at[c], recv_sem=recv_side.at[c],
        device_id={"orb": sibling(orb)}, device_id_type=MESH) for c in range(CHUNKS)]
    on = [pltpu.make_async_remote_copy(
        src_ref=onward[c], dst_ref=behind[c], send_sem=send_on.at[c], recv_sem=recv_on.at[c],
        device_id={"orb": lax.rem(orb + 2, orbs)}, device_id_type=MESH) for c in range(CHUNKS)]
    live = [jnp.where(slot < count[0], 1.0, 0.0) for slot in range(GRP * TURNS)]

    def summed(c, a, which, far):
        value = jnp.zeros((CHUNK, 128), jnp.float32)
        for slot in range(GRP * TURNS):
            term = landed[c][slot % GRP, slot // GRP, which]
            if which == 0:
                weight = jnp.where(first[slot] == a, live[slot], 0.0)
            else:
                weight = jnp.where((second[slot] == a) & (reach[slot] == far), live[slot], 0.0)
            value = value + weight * term
        return value

    for c in range(CHUNKS):
        landed[c][me] = terms[:, :, me, rows(c)]
    for c in range(CHUNKS):
        for copy in moved[c]:
            copy.wait_recv()
        for a in range(FRAG):
            aside[c][a] = summed(c, a, 1, 1)
        side[c].start()
        for a in range(FRAG):
            onward[c][a] = summed(c, a, 1, 2)
            action_ref[a, CHUNK * c:CHUNK * c + CHUNK, :] = summed(c, a, 0, 0) + summed(c, a, 1, 0)
        side[c].wait_recv()
        for a in range(FRAG):
            onward[c][a] = onward[c][a] + even * beside[c][a]
        on[c].start()
    products[...] = jnp.zeros_like(products)
    for c in range(CHUNKS):
        on[c].wait_recv()
        for b in range(FRAG):
            value = action_ref[b, CHUNK * c:CHUNK * c + CHUNK, :] + behind[c][b] + (1.0 - even) * beside[c][b]
            action_ref[b, CHUNK * c:CHUNK * c + CHUNK, :] = value
            for a in range(FRAG):
                part = jnp.sum((phi_ref[a, CHUNK * c:CHUNK * c + CHUNK, :] * value).reshape(CHUNK // 8, 8, 128), axis=0)
                products[b, a] = products[b, a] + part
    lane = lax.broadcasted_iota(jnp.int32, (FRAG, 128), 1)
    total = jnp.zeros((FRAG, 128), jnp.float32)
    for b in range(FRAG):
        part = jnp.sum(jnp.sum(products[b], axis=1), axis=1, keepdims=True)
        total = total + jnp.where(lane == b, part, 0.0)
    block[...] = total
    sums = []
    for step in range(1, GRP):
        sums.append(pltpu.make_async_remote_copy(
            src_ref=block, dst_ref=blocks.at[step], send_sem=send_sum.at[step], recv_sem=recv_sum.at[step],
            device_id={"grp": lax.rem(me + step, GRP)}, device_id_type=MESH))
        sums[-1].start()
    for c in range(CHUNKS):
        for copy in moved[c] + [side[c], on[c]]:
            copy.wait_send()
    for copy in sums:
        copy.wait()
    total_ref[...] = ((block[...] + blocks[2]) + (blocks[1] + blocks[3])) / float(B**3)


def collect(terms, phi, count, first, second, reach):
    vmem, smem = pl.BlockSpec(memory_space=pltpu.VMEM), pl.BlockSpec(memory_space=pltpu.SMEM)
    dma = pltpu.SemaphoreType.DMA
    return pl.pallas_call(
        collect_kernel,
        out_shape=(jax.ShapeDtypeStruct((FRAG, SLAB, 128), jnp.float32),
                   jax.ShapeDtypeStruct((FRAG, 128), jnp.float32)),
        in_specs=[vmem] * 2 + [smem] * 4,
        out_specs=(vmem, vmem),
        scratch_shapes=[pltpu.VMEM((GRP, TURNS, 2, CHUNK, 128), jnp.float32)] * CHUNKS
        + [pltpu.VMEM((FRAG, CHUNK, 128), jnp.float32)] * (4 * CHUNKS)
        + [pltpu.VMEM((FRAG, FRAG, 8, 128), jnp.float32),
           pltpu.VMEM((FRAG, 128), jnp.float32),
           pltpu.VMEM((GRP, FRAG, 128), jnp.float32),
           dma((CHUNKS, GRP)), dma((CHUNKS, GRP)), dma((CHUNKS,)), dma((CHUNKS,)), dma((CHUNKS,)), dma((CHUNKS,)),
           dma((GRP,)), dma((GRP,))],
        compiler_params=pltpu.CompilerParams(collective_id=1, has_side_effects=True, vmem_limit_bytes=40 << 20),
        name="collect",
    )(terms, phi, count, first, second, reach)


def project_kernel(phi_ref, action_ref, total_ref, gradient_ref, lagrange_ref, flat):
    total = total_ref[...][:, 0:FRAG]
    lagrange = 0.5 * (total + total.T)
    lagrange_ref[0] = lagrange
    for a in range(FRAG):
        value = action_ref[a]
        for b in range(FRAG):
            value = value - lagrange[b:b + 1, a:a + 1] * phi_ref[b]
        flat[SLAB * a:SLAB * a + SLAB, :] = value
    for x in range(12):
        for t in range(TILES):
            gradient_ref[FRAG * x:FRAG * x + FRAG, 128 * t:128 * t + 128] = flat[pl.ds(TILES * x + t, FRAG, stride=SLAB), :]


def projected(phi, action, total):
    vmem = pl.BlockSpec(memory_space=pltpu.VMEM)
    return pl.pallas_call(
        project_kernel,
        out_shape=(jax.ShapeDtypeStruct((12 * FRAG, B * B), jnp.float32),
                   jax.ShapeDtypeStruct((1, FRAG, FRAG), jnp.float32)),
        in_specs=[vmem] * 3,
        out_specs=(vmem, vmem),
        scratch_shapes=[pltpu.VMEM((FRAG * SLAB, 128), jnp.float32)],
        compiler_params=pltpu.CompilerParams(vmem_limit_bytes=40 << 20),
        name="projected",
    )(phi, action, total)


def shards(orbitals, kernel, anchors, pair_count, pair_first, pair_second, pair_reach):
    modes = mode_table(kernel)
    mine = orbitals.reshape(2, GRP, SLAB, 128)
    phi, pairs = spread(mine, pair_first, pair_second, pair_reach)
    terms = pair_terms(pairs, modes, anchors, pair_reach).reshape(TURNS, 2, GRP, SLAB, 128)
    action, total = collect(terms, phi, pair_count, pair_first, pair_second, pair_reach)
    gradient, lagrange = projected(phi, action, total)
    return gradient.reshape(12, FRAG, B * B).transpose(1, 0, 2), lagrange


def solution(mesh):
    placed = (P(("orb", "grp"), None, None), P(), P(), P("orb"), P("orb"), P("orb"), P("orb"))
    return jax.shard_map(
        shards,
        mesh=mesh,
        in_specs=placed,
        out_specs=(P("orb", "grp", None), P("orb", None, None)),
        check_vma=False,
    )
```

```python
import functools
import math

import jax
import jax.numpy as jnp
import ml_dtypes
import numpy as np
from jax import lax
from jax.experimental import pallas as pl
from jax.experimental.pallas import tpu as pltpu
from jax.sharding import PartitionSpec as P

MESH = pl.DeviceIdType.MESH
B = 48
FRAG = 8
GRP = 4
TURNS = 2
TILES = 18
SLAB = 216
ROWS = 864
HALF = 25
CH = 152
PADX = 16
PADT = 8
CHUNKS = 9
CHUNK = SLAB // CHUNKS


def split(a):
    a = a.astype(np.float32)
    head = a.astype(ml_dtypes.bfloat16)
    tail = (a - head.astype(np.float32)).astype(ml_dtypes.bfloat16)
    return head, tail


@functools.lru_cache(None)
def tables():
    c, kx = np.meshgrid(np.arange(6), np.arange(HALF), indexing="ij")
    c, kx = c.reshape(-1, 1), kx.reshape(-1, 1)
    a, x = np.meshgrid(np.arange(6), np.arange(B), indexing="ij")
    a, x = a.reshape(1, -1), x.reshape(1, -1)
    theta = 2 * np.pi * ((8 * c * a + kx * x) % 48) / 48
    left = np.zeros((2 * CH, 288))
    left[:150] = np.cos(theta)
    left[CH:CH + 150] = -np.sin(theta)
    left = np.concatenate(split(left), axis=1)
    inverse = np.concatenate([left[:, :288].T, left[:, 288:].T], axis=1)
    b, z = np.meshgrid(np.arange(8), np.arange(B), indexing="ij")
    b, z = b.reshape(-1), z.reshape(-1)
    phi = 2 * np.pi * ((6 * np.outer(b, b) + np.outer(z, z)) % 48) / 48
    right = np.concatenate(split(np.concatenate([np.cos(phi), -np.sin(phi)], axis=1)), axis=0)
    turn = 2 * np.pi * ((np.arange(6)[:, None] * b[None, :]) % 48) / 48
    twiddle = np.stack([np.cos(turn), -np.sin(turn)]).astype(np.float32)
    return left, inverse, right, twiddle


def halves(value):
    head = value.astype(jnp.bfloat16)
    return head, (value - head.astype(jnp.float32)).astype(jnp.bfloat16)


def dot(a, b):
    return jnp.dot(a, b, preferred_element_type=jnp.float32)


def modes_kernel(kernel_ref, modes_ref, picked, mirrored):
    for c in range(6):
        for e in range(8):
            picked[48 * c:48 * c + 48, 48 * e:48 * e + 48] = kernel_ref[:, 48 * (c + 6 * e):48 * (c + 6 * e) + 48]
    lane = lax.broadcasted_iota(jnp.int32, (1, 384), 1)
    e, kz = lane // B, lane % B
    row = lax.broadcasted_iota(jnp.int32, (384, 384), 0)
    for shift, rows in ((0, slice(0, 48)), (1, slice(48, 288))):
        source = (16 - e - shift) % 8 * B + (B - kz) % B
        permute = jnp.where(row == source, 1.0, 0.0).astype(jnp.bfloat16)
        head, tail = halves(picked[rows, :])
        mirrored[rows, :] = dot(head, permute) + dot(tail, permute)
    out = lax.broadcasted_iota(jnp.int32, (32, B), 0)
    permute = jnp.where(lax.broadcasted_iota(jnp.int32, (32, B), 1) == (B - out) % B, 1.0, 0.0).astype(jnp.bfloat16)
    kx = lax.broadcasted_iota(jnp.int32, (32, 384), 0)
    weight = jnp.where((kx == 0) | (kx == HALF - 1), 0.5 / B**3, 1.0 / B**3)
    modes_ref[144:CH, :] = jnp.zeros((8, 384), jnp.float32)
    for c in range(6):
        other = (6 - c) % 6
        head, tail = halves(mirrored[48 * other:48 * other + 48, :])
        even = (picked[48 * c:48 * c + 32, :] + dot(permute, head) + dot(permute, tail)) * weight
        modes_ref[HALF * c:HALF * c + HALF, :] = even[:HALF]


def mode_table(kernel):
    vmem = pl.BlockSpec(memory_space=pltpu.VMEM)
    return pl.pallas_call(
        modes_kernel,
        out_shape=jax.ShapeDtypeStruct((CH, 384), jnp.float32),
        in_specs=[vmem],
        out_specs=vmem,
        scratch_shapes=[pltpu.VMEM((288, 384), jnp.float32), pltpu.VMEM((288, 384), jnp.float32)],
        compiler_params=pltpu.CompilerParams(vmem_limit_bytes=6 << 20),
        name="mode_table",
    )(kernel)


def shifted(source, offset, emit):
    d0, d1, d2 = offset
    flat = 48 * d1 + d2 + 1024
    tile = lax.shift_right_logical(flat, 7) - 8
    lane_by = lax.bitwise_and(flat, 127)
    lane = lax.broadcasted_iota(jnp.int32, (B, 128), 1)
    late = lane >= lane_by
    insides = []
    for k in range(3):
        z = lax.rem(lane + 128 * k, B) - d2
        insides.append((z >= 0) & (z < B))
    before = None
    for t in range(-1, TILES):
        block = source[t - tile + PADT, pl.ds(PADX - d0, B), :]
        block = pltpu.roll(block, lane_by, 1)
        if t >= 0:
            emit(t, jnp.where(insides[t % 3], jnp.where(late, block, before), 0.0))
        before = block


def pair_kernel(pairs_ref, modes_ref, left_ref, inverse_ref, right_ref, twiddle_ref, anchors, reach_ref,
                out_ref, padded, moved, stack, wide, spec, volume, left, inverse, right, twiddle):
    left[:, 0:288] = left_ref[:, 0:288]
    left[:, 288:864] = left_ref[...]
    inverse[:, 0:304] = inverse_ref[:, 0:304]
    inverse[:, 304:912] = inverse_ref[...]
    right[0:384, :] = right_ref[0:384, :]
    right[384:1152, :] = right_ref[...]
    for c in range(6):
        rows = slice(HALF * c, HALF * c + HALF + 2 * (c == 5))
        for part in range(2):
            twiddle[part, rows, :] = jnp.broadcast_to(twiddle_ref[part, c:c + 1, :], (rows.stop - rows.start, 384))
    frag, member = lax.axis_index("orb"), lax.axis_index("grp")

    def offset_of(turn):
        partner = lax.rem(frag + reach_ref[member + GRP * turn], lax.axis_size("orb"))
        return [anchors[k, partner] - anchors[k, frag] for k in range(3)]

    padded[...] = jnp.zeros_like(padded)

    def at(t):
        return slice(48 * (t // 3), 48 * (t // 3) + 48), slice(128 * (t % 3), 128 * (t % 3) + 128)

    for turn in range(TURNS):
        for t in range(TILES):
            padded[t + PADT, pl.ds(PADX, B), :] = pairs_ref[turn, 1, pl.ds(t, B, stride=TILES), :]

        def emit(t, block):
            moved[turn, t] = block
            density = pairs_ref[turn, 0, pl.ds(t, B, stride=TILES), :] * block
            head, tail = halves(density)
            rows, lanes = at(t)
            lanes = slice(384 * turn + lanes.start, 384 * turn + lanes.stop)
            stack[rows.start:rows.stop, lanes] = head
            stack[288 + rows.start:288 + rows.stop, lanes] = tail
            stack[576 + rows.start:576 + rows.stop, lanes] = head

        shifted(padded, offset_of(turn), emit)

    volume[0:2 * CH, :] = dot(left[...], stack[0:864, :])
    tr, ti = twiddle[0], twiddle[1]

    def put(row, value):
        head, tail = halves(value)
        wide[row:row + CH, 0:384] = head
        wide[row:row + CH, 384:768] = tail
        wide[row:row + CH, 768:1152] = head

    for turn in range(TURNS):
        re = volume[0:CH, 384 * turn:384 * turn + 384]
        im = volume[CH:2 * CH, 384 * turn:384 * turn + 384]
        put(2 * CH * turn, re * tr - im * ti)
        put(2 * CH * turn + CH, re * ti + im * tr)
    spec[...] = dot(wide[...], right[...])
    table = modes_ref[...]
    for turn in range(TURNS):
        row = 2 * CH * turn
        re = spec[row:row + CH, 0:384] - spec[row + CH:row + 2 * CH, 384:768]
        im = spec[row:row + CH, 384:768] + spec[row + CH:row + 2 * CH, 0:384]
        put(row, re * table)
        put(row + CH, im * table)
    spec[...] = dot(wide[...], right[...])
    for turn in range(TURNS):
        row = 2 * CH * turn
        re = spec[row:row + CH, 0:384] + spec[row + CH:row + 2 * CH, 384:768]
        im = spec[row + CH:row + 2 * CH, 0:384] - spec[row:row + CH, 384:768]
        lanes = slice(384 * turn, 384 * turn + 384)
        for part, value in enumerate((re * tr + im * ti, im * tr - re * ti)):
            head, tail = halves(value)
            stack[CH * part:CH * part + CH, lanes] = head
            stack[304 + CH * part:304 + CH * part + CH, lanes] = tail
            stack[608 + CH * part:608 + CH * part + CH, lanes] = head
    volume[0:288, :] = dot(inverse[...], stack[...])

    for turn in range(TURNS):
        for t in range(TILES):
            rows, lanes = at(t)
            potential = volume[rows, 384 * turn + lanes.start:384 * turn + lanes.stop]
            out_ref[turn, 0, pl.ds(t, B, stride=TILES), :] = potential * moved[turn, t]
            padded[t + PADT, pl.ds(PADX, B), :] = potential * pairs_ref[turn, 0, pl.ds(t, B, stride=TILES), :]

        def emit(t, block):
            out_ref[turn, 1, pl.ds(t, B, stride=TILES), :] = block

        shifted(padded, [-d for d in offset_of(turn)], emit)


def pair_terms(pairs, modes, anchors, reach):
    left, inverse, right, twiddle = tables()
    vmem, smem = pl.BlockSpec(memory_space=pltpu.VMEM), pl.BlockSpec(memory_space=pltpu.SMEM)
    return pl.pallas_call(
        pair_kernel,
        out_shape=jax.ShapeDtypeStruct((TURNS, 2, ROWS, 128), jnp.float32),
        in_specs=[vmem] * 6 + [smem] * 2,
        out_specs=vmem,
        scratch_shapes=[
            pltpu.VMEM((TILES + 2 * PADT, B + 2 * PADX, 128), jnp.float32),
            pltpu.VMEM((TURNS, TILES, B, 128), jnp.float32),
            pltpu.VMEM((912, 768), jnp.bfloat16),
            pltpu.VMEM((2 * TURNS * CH, 1152), jnp.bfloat16),
            pltpu.VMEM((2 * TURNS * CH, 768), jnp.float32),
            pltpu.VMEM((2 * CH, 768), jnp.float32),
            pltpu.VMEM((2 * CH, 864), jnp.bfloat16),
            pltpu.VMEM((288, 912), jnp.bfloat16),
            pltpu.VMEM((1152, 768), jnp.bfloat16),
            pltpu.VMEM((2, CH, 384), jnp.float32),
        ],
        compiler_params=pltpu.CompilerParams(vmem_limit_bytes=24 << 20),
        name="pair_terms",
    )(pairs, modes, jnp.asarray(left), jnp.asarray(inverse), jnp.asarray(right), jnp.asarray(twiddle), anchors, reach)


def sibling(orb):
    return orb + 1 - 2 * lax.rem(orb, 2)


def greet(orb, member):
    barrier = pltpu.get_barrier_semaphore()
    orbs = lax.axis_size("orb")
    for step in range(1, GRP):
        pl.semaphore_signal(barrier, inc=1, device_id={"grp": lax.rem(member + step, GRP)}, device_id_type=MESH)
    for other in (sibling(orb), lax.rem(orb + 2, orbs), lax.rem(orb + orbs - 2, orbs)):
        pl.semaphore_signal(barrier, inc=1, device_id={"orb": other}, device_id_type=MESH)
    pl.semaphore_wait(barrier, GRP - 1 + 3)


def spread_kernel(mine, first, second, reach, phi_ref, pairs_ref, *scratch):
    near = scratch[0:3 * CHUNKS]
    out = scratch[3 * CHUNKS:5 * CHUNKS]
    send_slab, recv_slab, own_sem, send_ahead, recv_ahead, send_side, recv_side, send_pick, recv_pick = scratch[5 * CHUNKS:]
    orb, me = lax.axis_index("orb"), lax.axis_index("grp")
    orbs = lax.axis_size("orb")
    even = lax.rem(orb, 2) == 0
    behind = lax.rem(orb + orbs - 2, orbs)
    greet(orb, me)

    def rows(c):
        return pl.ds(CHUNK * c, CHUNK)

    slabs, owns = [], []
    for c in range(CHUNKS):
        group = []
        for step in (2, 1, 3):
            other = lax.rem(me + step, GRP)
            group.append(pltpu.make_async_remote_copy(
                src_ref=mine.at[:, other, rows(c)], dst_ref=near[3 * c].at[pl.ds(2 * me, 2)],
                send_sem=send_slab.at[c, step], recv_sem=recv_slab.at[c, step],
                device_id={"grp": other}, device_id_type=MESH))
        slabs.append(group)
        owns.append(pltpu.make_async_copy(mine.at[:, me, rows(c)], near[3 * c].at[pl.ds(2 * me, 2)], own_sem.at[c]))
        owns[c].start()
        for copy in group:
            copy.start()

    ahead = [pltpu.make_async_remote_copy(
        src_ref=near[3 * c], dst_ref=near[3 * c + 2], send_sem=send_ahead.at[c], recv_sem=recv_ahead.at[c],
        device_id={"orb": behind}, device_id_type=MESH) for c in range(CHUNKS)]
    side = [[pltpu.make_async_remote_copy(
        src_ref=near[3 * c + which], dst_ref=near[3 * c + 1], send_sem=send_side.at[c], recv_sem=recv_side.at[c],
        device_id={"orb": sibling(orb)}, device_id_type=MESH) for which in (2, 0)] for c in range(CHUNKS)]

    def picks(which, c):
        copies = []
        for step in (2, 1, 3):
            other = lax.rem(me + step, GRP)
            copies.append(pltpu.make_async_remote_copy(
                src_ref=out[2 * c + which].at[other],
                dst_ref=pairs_ref.at[:, which, pl.ds(SLAB * me + CHUNK * c, CHUNK)],
                send_sem=send_pick.at[which, c, step], recv_sem=recv_pick.at[which, c, step],
                device_id={"grp": other}, device_id_type=MESH))
        return copies

    picked = [[picks(which, c) for c in range(CHUNKS)] for which in range(2)]

    def choose(which, c):
        for slot in range(GRP * TURNS):
            if which == 0:
                value = near[3 * c][first[slot]]
            else:
                value = near[3 * c][second[slot]]
                value = jnp.where(reach[slot] == 1, near[3 * c + 1][second[slot]], value)
                value = jnp.where(reach[slot] == 2, near[3 * c + 2][second[slot]], value)
            out[2 * c + which][slot % GRP, slot // GRP] = value
        for copy in picked[which][c]:
            copy.start()
        pairs_ref[:, which, pl.ds(pl.multiple_of(SLAB * me + CHUNK * c, 8), CHUNK), :] = out[2 * c + which][me]

    for c in range(CHUNKS):
        owns[c].wait()
        for copy in slabs[c]:
            copy.wait_recv()
        ahead[c].start()

        @pl.when(jnp.logical_not(even))
        def _():
            side[c][1].start()

        choose(0, c)
        phi_ref[:, CHUNK * c:CHUNK * c + CHUNK, :] = near[3 * c][...]
    for c in range(CHUNKS + 1):
        if c < CHUNKS:
            ahead[c].wait_recv()

            @pl.when(even)
            def _():
                side[c][0].start()

        if c > 0:
            side[c - 1][0].wait_recv()
            choose(1, c - 1)
    for c in range(CHUNKS):
        for copy in slabs[c]:
            copy.wait_send()
        ahead[c].wait_send()

        @pl.when(even)
        def _():
            side[c][0].wait_send()

        @pl.when(jnp.logical_not(even))
        def _():
            side[c][1].wait_send()

        for which in range(2):
            for copy in picked[which][c]:
                copy.wait()


def spread(mine, first, second, reach):
    vmem, smem = pl.BlockSpec(memory_space=pltpu.VMEM), pl.BlockSpec(memory_space=pltpu.SMEM)
    dma = pltpu.SemaphoreType.DMA
    return pl.pallas_call(
        spread_kernel,
        out_shape=(jax.ShapeDtypeStruct((FRAG, SLAB, 128), jnp.float32),
                   jax.ShapeDtypeStruct((TURNS, 2, ROWS, 128), jnp.float32)),
        in_specs=[vmem] + [smem] * 3,
        out_specs=(vmem, vmem),
        scratch_shapes=[pltpu.VMEM((FRAG, CHUNK, 128), jnp.float32)] * (3 * CHUNKS)
        + [pltpu.VMEM((GRP, TURNS, CHUNK, 128), jnp.float32)] * (2 * CHUNKS)
        + [dma((CHUNKS, GRP)), dma((CHUNKS, GRP)), dma((CHUNKS,)), dma((CHUNKS,)), dma((CHUNKS,)),
           dma((CHUNKS,)), dma((CHUNKS,)), dma((2, CHUNKS, GRP)), dma((2, CHUNKS, GRP))],
        compiler_params=pltpu.CompilerParams(collective_id=0, has_side_effects=True, vmem_limit_bytes=14 << 20),
        name="spread",
    )(mine, first, second, reach)


def collect_kernel(terms, phi_ref, count, first, second, reach, action_ref, total_ref, *scratch):
    landed = scratch[0:CHUNKS]
    aside = scratch[CHUNKS:2 * CHUNKS]
    beside = scratch[2 * CHUNKS:3 * CHUNKS]
    onward = scratch[3 * CHUNKS:4 * CHUNKS]
    behind = scratch[4 * CHUNKS:5 * CHUNKS]
    (products, block, blocks, send_term, recv_term, send_side, recv_side, send_on, recv_on,
     send_sum, recv_sum) = scratch[5 * CHUNKS:]
    orb, me = lax.axis_index("orb"), lax.axis_index("grp")
    orbs = lax.axis_size("orb")
    even = jnp.where(lax.rem(orb, 2) == 0, 1.0, 0.0)
    greet(orb, me)

    def rows(c):
        return pl.ds(CHUNK * c, CHUNK)

    moved = []
    for c in range(CHUNKS):
        group = []
        for step in (2, 1, 3):
            other = lax.rem(me + step, GRP)
            group.append(pltpu.make_async_remote_copy(
                src_ref=terms.at[:, :, other, rows(c)], dst_ref=landed[c].at[me],
                send_sem=send_term.at[c, step], recv_sem=recv_term.at[c, step],
                device_id={"grp": other}, device_id_type=MESH))
        moved.append(group)
        for copy in group:
            copy.start()
    side = [pltpu.make_async_remote_copy(
        src_ref=aside[c], dst_ref=beside[c], send_sem=send_side.at[c], recv_sem=recv_side.at[c],
        device_id={"orb": sibling(orb)}, device_id_type=MESH) for c in range(CHUNKS)]
    on = [pltpu.make_async_remote_copy(
        src_ref=onward[c], dst_ref=behind[c], send_sem=send_on.at[c], recv_sem=recv_on.at[c],
        device_id={"orb": lax.rem(orb + 2, orbs)}, device_id_type=MESH) for c in range(CHUNKS)]
    live = [jnp.where(slot < count[0], 1.0, 0.0) for slot in range(GRP * TURNS)]

    def summed(c, a, which, far):
        value = jnp.zeros((CHUNK, 128), jnp.float32)
        for slot in range(GRP * TURNS):
            term = landed[c][slot % GRP, slot // GRP, which]
            if which == 0:
                weight = jnp.where(first[slot] == a, live[slot], 0.0)
            else:
                weight = jnp.where((second[slot] == a) & (reach[slot] == far), live[slot], 0.0)
            value = value + weight * term
        return value

    for c in range(CHUNKS):
        landed[c][me] = terms[:, :, me, rows(c)]
    for c in range(CHUNKS):
        for copy in moved[c]:
            copy.wait_recv()
        for a in range(FRAG):
            aside[c][a] = summed(c, a, 1, 1)
        side[c].start()
        for a in range(FRAG):
            onward[c][a] = summed(c, a, 1, 2)
            action_ref[a, CHUNK * c:CHUNK * c + CHUNK, :] = summed(c, a, 0, 0) + summed(c, a, 1, 0)
        side[c].wait_recv()
        for a in range(FRAG):
            onward[c][a] = onward[c][a] + even * beside[c][a]
        on[c].start()
    products[...] = jnp.zeros_like(products)
    for c in range(CHUNKS):
        on[c].wait_recv()
        for b in range(FRAG):
            value = action_ref[b, CHUNK * c:CHUNK * c + CHUNK, :] + behind[c][b] + (1.0 - even) * beside[c][b]
            action_ref[b, CHUNK * c:CHUNK * c + CHUNK, :] = value
            for a in range(FRAG):
                part = jnp.sum((phi_ref[a, CHUNK * c:CHUNK * c + CHUNK, :] * value).reshape(CHUNK // 8, 8, 128), axis=0)
                products[b, a] = products[b, a] + part
    lane = lax.broadcasted_iota(jnp.int32, (FRAG, 128), 1)
    total = jnp.zeros((FRAG, 128), jnp.float32)
    for b in range(FRAG):
        part = jnp.sum(jnp.sum(products[b], axis=1), axis=1, keepdims=True)
        total = total + jnp.where(lane == b, part, 0.0)
    block[...] = total
    sums = []
    for step in range(1, GRP):
        sums.append(pltpu.make_async_remote_copy(
            src_ref=block, dst_ref=blocks.at[step], send_sem=send_sum.at[step], recv_sem=recv_sum.at[step],
            device_id={"grp": lax.rem(me + step, GRP)}, device_id_type=MESH))
        sums[-1].start()
    for c in range(CHUNKS):
        for copy in moved[c] + [side[c], on[c]]:
            copy.wait_send()
    for copy in sums:
        copy.wait()
    total_ref[...] = ((block[...] + blocks[2]) + (blocks[1] + blocks[3])) / float(B**3)


def collect(terms, phi, count, first, second, reach):
    vmem, smem = pl.BlockSpec(memory_space=pltpu.VMEM), pl.BlockSpec(memory_space=pltpu.SMEM)
    dma = pltpu.SemaphoreType.DMA
    return pl.pallas_call(
        collect_kernel,
        out_shape=(jax.ShapeDtypeStruct((FRAG, SLAB, 128), jnp.float32),
                   jax.ShapeDtypeStruct((FRAG, 128), jnp.float32)),
        in_specs=[vmem] * 2 + [smem] * 4,
        out_specs=(vmem, vmem),
        scratch_shapes=[pltpu.VMEM((GRP, TURNS, 2, CHUNK, 128), jnp.float32)] * CHUNKS
        + [pltpu.VMEM((FRAG, CHUNK, 128), jnp.float32)] * (4 * CHUNKS)
        + [pltpu.VMEM((FRAG, FRAG, 8, 128), jnp.float32),
           pltpu.VMEM((FRAG, 128), jnp.float32),
           pltpu.VMEM((GRP, FRAG, 128), jnp.float32),
           dma((CHUNKS, GRP)), dma((CHUNKS, GRP)), dma((CHUNKS,)), dma((CHUNKS,)), dma((CHUNKS,)), dma((CHUNKS,)),
           dma((GRP,)), dma((GRP,))],
        compiler_params=pltpu.CompilerParams(collective_id=1, has_side_effects=True, vmem_limit_bytes=14 << 20),
        name="collect",
    )(terms, phi, count, first, second, reach)


def project_kernel(phi_ref, action_ref, total_ref, gradient_ref, lagrange_ref, flat):
    total = total_ref[...][:, 0:FRAG]
    lagrange = 0.5 * (total + total.T)
    lagrange_ref[0] = lagrange
    for a in range(FRAG):
        value = action_ref[a]
        for b in range(FRAG):
            value = value - lagrange[b:b + 1, a:a + 1] * phi_ref[b]
        flat[SLAB * a:SLAB * a + SLAB, :] = value
    for x in range(12):
        for t in range(TILES):
            gradient_ref[FRAG * x:FRAG * x + FRAG, 128 * t:128 * t + 128] = flat[pl.ds(TILES * x + t, FRAG, stride=SLAB), :]


def projected(phi, action, total):
    vmem = pl.BlockSpec(memory_space=pltpu.VMEM)
    return pl.pallas_call(
        project_kernel,
        out_shape=(jax.ShapeDtypeStruct((12 * FRAG, B * B), jnp.float32),
                   jax.ShapeDtypeStruct((1, FRAG, FRAG), jnp.float32)),
        in_specs=[vmem] * 3,
        out_specs=(vmem, vmem),
        scratch_shapes=[pltpu.VMEM((FRAG * SLAB, 128), jnp.float32)],
        compiler_params=pltpu.CompilerParams(vmem_limit_bytes=8 << 20),
        name="projected",
    )(phi, action, total)


def shards(orbitals, kernel, anchors, pair_count, pair_first, pair_second, pair_reach):
    modes = mode_table(kernel)
    mine = orbitals.reshape(2, GRP, SLAB, 128)
    phi, pairs = spread(mine, pair_first, pair_second, pair_reach)
    terms = pair_terms(pairs, modes, anchors.T, pair_reach).reshape(TURNS, 2, GRP, SLAB, 128)
    action, total = collect(terms, phi, pair_count, pair_first, pair_second, pair_reach)
    gradient, lagrange = projected(phi, action, total)
    return gradient.reshape(12, FRAG, B * B).transpose(1, 0, 2), lagrange


def solution(mesh):
    placed = (P(("orb", "grp"), None, None), P(), P(), P("orb"), P("orb"), P("orb"), P("orb"))
    return jax.shard_map(
        shards,
        mesh=mesh,
        in_specs=placed,
        out_specs=(P("orb", "grp", None), P("orb", None, None)),
        check_vma=False,
    )
```

```python
import functools
import math

import jax
import jax.numpy as jnp
import ml_dtypes
import numpy as np
from jax import lax
from jax.experimental import pallas as pl
from jax.experimental.pallas import tpu as pltpu
from jax.sharding import PartitionSpec as P

MESH = pl.DeviceIdType.MESH
B = 48
FRAG = 8
GRP = 4
TURNS = 2
TILES = 18
SLAB = 216
ROWS = 864
HALF = 25
CH = 152
PADX = 16
PADT = 8
CHUNKS = 9
CHUNK = SLAB // CHUNKS


def split(a):
    a = a.astype(np.float32)
    head = a.astype(ml_dtypes.bfloat16)
    tail = (a - head.astype(np.float32)).astype(ml_dtypes.bfloat16)
    return head, tail


@functools.lru_cache(None)
def tables():
    c, kx = np.meshgrid(np.arange(6), np.arange(HALF), indexing="ij")
    c, kx = c.reshape(-1, 1), kx.reshape(-1, 1)
    a, x = np.meshgrid(np.arange(6), np.arange(B), indexing="ij")
    a, x = a.reshape(1, -1), x.reshape(1, -1)
    theta = 2 * np.pi * ((8 * c * a + kx * x) % 48) / 48
    left = np.zeros((2 * CH, 288))
    left[:150] = np.cos(theta)
    left[CH:CH + 150] = -np.sin(theta)
    left = np.concatenate(split(left), axis=1)
    inverse = np.concatenate([left[:, :288].T, left[:, 288:].T], axis=1)
    b, z = np.meshgrid(np.arange(8), np.arange(B), indexing="ij")
    b, z = b.reshape(-1), z.reshape(-1)
    phi = 2 * np.pi * ((6 * np.outer(b, b) + np.outer(z, z)) % 48) / 48
    right = np.concatenate(split(np.concatenate([np.cos(phi), -np.sin(phi)], axis=1)), axis=0)
    turn = 2 * np.pi * ((np.arange(6)[:, None] * b[None, :]) % 48) / 48
    twiddle = np.stack([np.cos(turn), -np.sin(turn)]).astype(np.float32)
    return left, inverse, right, twiddle


def halves(value):
    head = value.astype(jnp.bfloat16)
    return head, (value - head.astype(jnp.float32)).astype(jnp.bfloat16)


def dot(a, b):
    return jnp.dot(a, b, preferred_element_type=jnp.float32)


def modes_of(kernel_ref, modes_ref, picked, mirrored):
    for c in range(6):
        for e in range(8):
            picked[48 * c:48 * c + 48, 48 * e:48 * e + 48] = kernel_ref[:, 48 * (c + 6 * e):48 * (c + 6 * e) + 48]
    lane = lax.broadcasted_iota(jnp.int32, (1, 384), 1)
    e, kz = lane // B, lane % B
    row = lax.broadcasted_iota(jnp.int32, (384, 384), 0)
    for shift, rows in ((0, slice(0, 48)), (1, slice(48, 288))):
        source = (16 - e - shift) % 8 * B + (B - kz) % B
        permute = jnp.where(row == source, 1.0, 0.0).astype(jnp.bfloat16)
        head, tail = halves(picked[rows, :])
        mirrored[rows, :] = dot(head, permute) + dot(tail, permute)
    out = lax.broadcasted_iota(jnp.int32, (32, B), 0)
    permute = jnp.where(lax.broadcasted_iota(jnp.int32, (32, B), 1) == (B - out) % B, 1.0, 0.0).astype(jnp.bfloat16)
    kx = lax.broadcasted_iota(jnp.int32, (32, 384), 0)
    weight = jnp.where((kx == 0) | (kx == HALF - 1), 0.5 / B**3, 1.0 / B**3)
    modes_ref[144:CH, :] = jnp.zeros((8, 384), jnp.float32)
    for c in range(6):
        other = (6 - c) % 6
        head, tail = halves(mirrored[48 * other:48 * other + 48, :])
        even = (picked[48 * c:48 * c + 32, :] + dot(permute, head) + dot(permute, tail)) * weight
        modes_ref[HALF * c:HALF * c + HALF, :] = even[:HALF]


def shifted(source, offset, emit):
    d0, d1, d2 = offset
    flat = 48 * d1 + d2 + 1024
    tile = lax.shift_right_logical(flat, 7) - 8
    lane_by = lax.bitwise_and(flat, 127)
    lane = lax.broadcasted_iota(jnp.int32, (B, 128), 1)
    late = lane >= lane_by
    insides = []
    for k in range(3):
        z = lax.rem(lane + 128 * k, B) - d2
        insides.append((z >= 0) & (z < B))
    before = None
    for t in range(-1, TILES):
        block = source[t - tile + PADT, pl.ds(PADX - d0, B), :]
        block = pltpu.roll(block, lane_by, 1)
        if t >= 0:
            emit(t, jnp.where(insides[t % 3], jnp.where(late, block, before), 0.0))
        before = block


def stack_tables(left_ref, inverse_ref, right_ref, twiddle_ref, left, inverse, right, twiddle):
    left[:, 0:288] = left_ref[:, 0:288]
    left[:, 288:864] = left_ref[...]
    inverse[:, 0:304] = inverse_ref[:, 0:304]
    inverse[:, 304:912] = inverse_ref[...]
    right[0:384, :] = right_ref[0:384, :]
    right[384:1152, :] = right_ref[...]
    for c in range(6):
        rows = slice(HALF * c, HALF * c + HALF + 2 * (c == 5))
        for part in range(2):
            twiddle[part, rows, :] = jnp.broadcast_to(twiddle_ref[part, c:c + 1, :], (rows.stop - rows.start, 384))


def block_of(t):
    return slice(48 * (t // 3), 48 * (t // 3) + 48), slice(128 * (t % 3), 128 * (t % 3) + 128)


def potentials(pairs, offsets, modes, left, inverse, right, twiddle, padded, moved, stack, wide, spec, volume):
    for turn in range(TURNS):
        for t in range(TILES):
            padded[t + PADT, pl.ds(PADX, B), :] = pairs[turn, 1, pl.ds(t, B, stride=TILES), :]

        def emit(t, block):
            moved[turn, t] = block
            density = pairs[turn, 0, pl.ds(t, B, stride=TILES), :] * block
            head, tail = halves(density)
            rows, lanes = block_of(t)
            lanes = slice(384 * turn + lanes.start, 384 * turn + lanes.stop)
            stack[rows.start:rows.stop, lanes] = head
            stack[288 + rows.start:288 + rows.stop, lanes] = tail
            stack[576 + rows.start:576 + rows.stop, lanes] = head

        shifted(padded, offsets[turn], emit)

    volume[0:2 * CH, :] = dot(left[...], stack[0:864, :])
    tr, ti = twiddle[0], twiddle[1]

    def put(row, value):
        head, tail = halves(value)
        wide[row:row + CH, 0:384] = head
        wide[row:row + CH, 384:768] = tail
        wide[row:row + CH, 768:1152] = head

    for turn in range(TURNS):
        re = volume[0:CH, 384 * turn:384 * turn + 384]
        im = volume[CH:2 * CH, 384 * turn:384 * turn + 384]
        put(2 * CH * turn, re * tr - im * ti)
        put(2 * CH * turn + CH, re * ti + im * tr)
    spec[...] = dot(wide[...], right[...])
    table = modes[...]
    for turn in range(TURNS):
        row = 2 * CH * turn
        re = spec[row:row + CH, 0:384] - spec[row + CH:row + 2 * CH, 384:768]
        im = spec[row:row + CH, 384:768] + spec[row + CH:row + 2 * CH, 0:384]
        put(row, re * table)
        put(row + CH, im * table)
    spec[...] = dot(wide[...], right[...])
    for turn in range(TURNS):
        row = 2 * CH * turn
        re = spec[row:row + CH, 0:384] + spec[row + CH:row + 2 * CH, 384:768]
        im = spec[row + CH:row + 2 * CH, 0:384] - spec[row:row + CH, 384:768]
        lanes = slice(384 * turn, 384 * turn + 384)
        for part, value in enumerate((re * tr + im * ti, im * tr - re * ti)):
            head, tail = halves(value)
            stack[CH * part:CH * part + CH, lanes] = head
            stack[304 + CH * part:304 + CH * part + CH, lanes] = tail
            stack[608 + CH * part:608 + CH * part + CH, lanes] = head
    volume[0:288, :] = dot(inverse[...], stack[...])


def terms_of(turn, pairs, offset, volume, moved, padded, terms):
    for t in range(TILES):
        rows, lanes = block_of(t)
        potential = volume[rows, 384 * turn + lanes.start:384 * turn + lanes.stop]
        terms[turn, 0, pl.ds(t, B, stride=TILES), :] = potential * moved[turn, t]
        padded[t + PADT, pl.ds(PADX, B), :] = potential * pairs[turn, 0, pl.ds(t, B, stride=TILES), :]

    def emit(t, block):
        terms[turn, 1, pl.ds(t, B, stride=TILES), :] = block

    shifted(padded, [-d for d in offset], emit)


def sibling(orb):
    return orb + 1 - 2 * lax.rem(orb, 2)


def exchange_kernel(orbitals, kernel, left_hbm, inverse_hbm, right_hbm, twiddle_hbm, anchors_hbm, count_hbm, first_hbm,
                    second_hbm, reach_hbm, phi_ref, action_ref, total_ref, *scratch):
    scratch = list(scratch)

    def take(n):
        taken, scratch[:] = scratch[:n], scratch[n:]
        return taken

    near = take(3 * CHUNKS)
    out = take(2 * CHUNKS)
    landed, aside, beside, onward, behind = (take(CHUNKS) for _ in range(5))
    native, kernel_ref, left_ref, inverse_ref, right_ref, twiddle_ref = take(6)
    anchors, count, first, second, reach = take(5)
    mine, pairs, terms, modes, picked, mirrored, left, inverse, right, twiddle = take(10)
    padded, moved, stack, wide, spec, volume = take(6)
    products, block, blocks = take(3)
    (load_sem, send_slab, recv_slab, own_sem, send_ahead, recv_ahead, send_side, recv_side, send_pick, recv_pick,
     send_term, recv_term, send_back, recv_back, send_on, recv_on, send_sum, recv_sum) = scratch
    orb, me = lax.axis_index("orb"), lax.axis_index("grp")
    orbs = lax.axis_size("orb")
    even = lax.rem(orb, 2) == 0
    is_even = jnp.where(even, 1.0, 0.0)
    sources = (orbitals, first_hbm, second_hbm, reach_hbm, kernel, left_hbm, inverse_hbm, right_hbm, twiddle_hbm,
               anchors_hbm, count_hbm)
    places = (native, first, second, reach, kernel_ref, left_ref, inverse_ref, right_ref, twiddle_ref, anchors, count)
    loads = [pltpu.make_async_copy(s, p, load_sem.at[i]) for i, (s, p) in enumerate(zip(sources, places))]
    for load in loads:
        load.start()
    barrier = pltpu.get_barrier_semaphore()
    for step in range(1, GRP):
        pl.semaphore_signal(barrier, inc=1, device_id={"grp": lax.rem(me + step, GRP)}, device_id_type=MESH)
    for other in (sibling(orb), lax.rem(orb + 2, orbs), lax.rem(orb + orbs - 2, orbs)):
        pl.semaphore_signal(barrier, inc=1, device_id={"orb": other}, device_id_type=MESH)
    loads[0].wait()
    for j in range(2):
        for t in range(TILES):
            mine[j, pl.ds(t, B, stride=TILES), :] = native[j, :, 128 * t:128 * t + 128]
    pl.semaphore_wait(barrier, GRP - 1 + 3)

    def rows(c):
        return pl.ds(CHUNK * c, CHUNK)

    def peers():
        return [(step, lax.rem(me + step, GRP)) for step in (2, 1, 3)]

    def at_slab(member, c):
        return pl.ds(pl.multiple_of(SLAB * member + CHUNK * c, 8), CHUNK)

    slabs, owns = [], []
    for c in range(CHUNKS):
        slabs.append([pltpu.make_async_remote_copy(
            src_ref=mine.at[:, at_slab(other, c)], dst_ref=near[3 * c].at[pl.ds(2 * me, 2)],
            send_sem=send_slab.at[c, step], recv_sem=recv_slab.at[c, step],
            device_id={"grp": other}, device_id_type=MESH) for step, other in peers()])
        owns.append(pltpu.make_async_copy(mine.at[:, at_slab(me, c)], near[3 * c].at[pl.ds(2 * me, 2)], own_sem.at[c]))
        owns[c].start()
        for copy in slabs[c]:
            copy.start()

    ahead = [pltpu.make_async_remote_copy(
        src_ref=near[3 * c], dst_ref=near[3 * c + 2], send_sem=send_ahead.at[c], recv_sem=recv_ahead.at[c],
        device_id={"orb": lax.rem(orb + orbs - 2, orbs)}, device_id_type=MESH) for c in range(CHUNKS)]
    side = [[pltpu.make_async_remote_copy(
        src_ref=near[3 * c + which], dst_ref=near[3 * c + 1], send_sem=send_side.at[c], recv_sem=recv_side.at[c],
        device_id={"orb": sibling(orb)}, device_id_type=MESH) for which in (2, 0)] for c in range(CHUNKS)]
    picks = [[[pltpu.make_async_remote_copy(
        src_ref=out[2 * c + which].at[other], dst_ref=pairs.at[:, which, at_slab(me, c)],
        send_sem=send_pick.at[which, c, step], recv_sem=recv_pick.at[which, c, step],
        device_id={"grp": other}, device_id_type=MESH) for step, other in peers()]
        for c in range(CHUNKS)] for which in range(2)]

    def choose(which, c):
        for slot in range(GRP * TURNS):
            if which == 0:
                value = near[3 * c][first[slot]]
            else:
                value = near[3 * c][second[slot]]
                value = jnp.where(reach[slot] == 1, near[3 * c + 1][second[slot]], value)
                value = jnp.where(reach[slot] == 2, near[3 * c + 2][second[slot]], value)
            out[2 * c + which][slot % GRP, slot // GRP] = value
        for copy in picks[which][c]:
            copy.start()
        pairs[:, which, at_slab(me, c), :] = out[2 * c + which][me]

    for load in loads[1:4]:
        load.wait()
    for c in range(CHUNKS):
        owns[c].wait()
        for copy in slabs[c]:
            copy.wait_recv()
        ahead[c].start()

        @pl.when(jnp.logical_not(even))
        def _():
            side[c][1].start()

        choose(0, c)
        phi_ref[:, CHUNK * c:CHUNK * c + CHUNK, :] = near[3 * c][...]
        if c == 0:
            for load in loads[4:]:
                load.wait()
            stack_tables(left_ref, inverse_ref, right_ref, twiddle_ref, left, inverse, right, twiddle)
        if c == 1:
            modes_of(kernel_ref, modes, picked, mirrored)
        if c == 2:
            padded[...] = jnp.zeros_like(padded)
    for c in range(CHUNKS + 1):
        if c < CHUNKS:
            ahead[c].wait_recv()

            @pl.when(even)
            def _():
                side[c][0].start()

        if c > 0:
            side[c - 1][0].wait_recv()
            choose(1, c - 1)
    for c in range(CHUNKS):
        for which in range(2):
            for copy in picks[which][c]:
                copy.wait_recv()

    offsets = []
    for turn in range(TURNS):
        far = reach[me + GRP * turn]
        offsets.append([anchors[k, lax.rem(orb + far, orbs)] - anchors[k, orb] for k in range(3)])
    potentials(pairs, offsets, modes, left, inverse, right, twiddle, padded, moved, stack, wide, spec, volume)

    sends = [[[pltpu.make_async_remote_copy(
        src_ref=terms.at[turn, :, at_slab(other, c)], dst_ref=landed[c].at[me, turn],
        send_sem=send_term.at[turn, c, step], recv_sem=recv_term.at[turn, c, step],
        device_id={"grp": other}, device_id_type=MESH) for step, other in peers()]
        for c in range(CHUNKS)] for turn in range(TURNS)]
    early = 2
    for turn in range(TURNS):
        terms_of(turn, pairs, offsets[turn], volume, moved, padded, terms)
        for c in range(CHUNKS):
            for other_turn in range(TURNS):
                if turn == (0 if other_turn == 0 and c < early else 1):
                    for copy in sends[other_turn][c]:
                        copy.start()
    back = [pltpu.make_async_remote_copy(
        src_ref=aside[c], dst_ref=beside[c], send_sem=send_back.at[c], recv_sem=recv_back.at[c],
        device_id={"orb": sibling(orb)}, device_id_type=MESH) for c in range(CHUNKS)]
    on = [pltpu.make_async_remote_copy(
        src_ref=onward[c], dst_ref=behind[c], send_sem=send_on.at[c], recv_sem=recv_on.at[c],
        device_id={"orb": lax.rem(orb + 2, orbs)}, device_id_type=MESH) for c in range(CHUNKS)]
    live = [jnp.where(slot < count[0], 1.0, 0.0) for slot in range(GRP * TURNS)]

    def summed(c, a, which, far):
        value = jnp.zeros((CHUNK, 128), jnp.float32)
        for slot in range(GRP * TURNS):
            term = landed[c][slot % GRP, slot // GRP, which]
            if which == 0:
                weight = jnp.where(first[slot] == a, live[slot], 0.0)
            else:
                weight = jnp.where((second[slot] == a) & (reach[slot] == far), live[slot], 0.0)
            value = value + weight * term
        return value

    for c in range(CHUNKS):
        landed[c][me] = terms[:, :, at_slab(me, c), :]
    for c in range(CHUNKS):
        for turn in range(TURNS):
            for copy in sends[turn][c]:
                copy.wait_recv()
        for a in range(FRAG):
            aside[c][a] = summed(c, a, 1, 1)
        back[c].start()
        for a in range(FRAG):
            onward[c][a] = summed(c, a, 1, 2)
            action_ref[a, CHUNK * c:CHUNK * c + CHUNK, :] = summed(c, a, 0, 0) + summed(c, a, 1, 0)
        back[c].wait_recv()
        for a in range(FRAG):
            onward[c][a] = onward[c][a] + is_even * beside[c][a]
        on[c].start()
    products[...] = jnp.zeros_like(products)
    for c in range(CHUNKS):
        on[c].wait_recv()
        for b in range(FRAG):
            value = action_ref[b, CHUNK * c:CHUNK * c + CHUNK, :] + behind[c][b] + (1.0 - is_even) * beside[c][b]
            action_ref[b, CHUNK * c:CHUNK * c + CHUNK, :] = value
            for a in range(FRAG):
                part = jnp.sum((phi_ref[a, CHUNK * c:CHUNK * c + CHUNK, :] * value).reshape(CHUNK // 8, 8, 128), axis=0)
                products[b, a] = products[b, a] + part
    lane = lax.broadcasted_iota(jnp.int32, (FRAG, 128), 1)
    total = jnp.zeros((FRAG, 128), jnp.float32)
    for b in range(FRAG):
        part = jnp.sum(jnp.sum(products[b], axis=1), axis=1, keepdims=True)
        total = total + jnp.where(lane == b, part, 0.0)
    block[...] = total
    sums = []
    for step, other in peers():
        sums.append(pltpu.make_async_remote_copy(
            src_ref=block, dst_ref=blocks.at[step], send_sem=send_sum.at[step], recv_sem=recv_sum.at[step],
            device_id={"grp": other}, device_id_type=MESH))
        sums[-1].start()
    for c in range(CHUNKS):
        for copy in slabs[c] + [ahead[c], back[c], on[c]] + [k for w in range(2) for k in picks[w][c] + sends[w][c]]:
            copy.wait_send()

        @pl.when(even)
        def _():
            side[c][0].wait_send()

        @pl.when(jnp.logical_not(even))
        def _():
            side[c][1].wait_send()

    for copy in sums:
        copy.wait()
    total_ref[...] = ((block[...] + blocks[2]) + (blocks[1] + blocks[3])) / float(B**3)


def exchange(orbitals, kernel, anchors, count, first, second, reach):
    left, inverse, right, twiddle = (jnp.asarray(t) for t in tables())
    vmem, hbm = pl.BlockSpec(memory_space=pltpu.VMEM), pl.BlockSpec(memory_space=pltpu.HBM)
    dma, f32, bf16 = pltpu.SemaphoreType.DMA, jnp.float32, jnp.bfloat16
    per_chunk, per_peer = dma((CHUNKS,)), dma((CHUNKS, GRP))
    part = pltpu.VMEM((FRAG, CHUNK, 128), f32)
    return pl.pallas_call(
        exchange_kernel,
        out_shape=(jax.ShapeDtypeStruct((FRAG, SLAB, 128), f32),
                   jax.ShapeDtypeStruct((FRAG, SLAB, 128), f32),
                   jax.ShapeDtypeStruct((FRAG, 128), f32)),
        in_specs=[hbm] * 11,
        out_specs=(vmem, vmem, vmem),
        scratch_shapes=[part] * (3 * CHUNKS)
        + [pltpu.VMEM((GRP, TURNS, CHUNK, 128), f32)] * (2 * CHUNKS)
        + [pltpu.VMEM((GRP, TURNS, 2, CHUNK, 128), f32)] * CHUNKS
        + [part] * (4 * CHUNKS)
        + [pltpu.VMEM(a.shape, a.dtype) for a in (orbitals, kernel, left, inverse, right, twiddle)]
        + [pltpu.SMEM(a.shape, a.dtype) for a in (anchors, count, first, second, reach)]
        + [pltpu.VMEM((2, ROWS, 128), f32),
           pltpu.VMEM((TURNS, 2, ROWS, 128), f32),
           pltpu.VMEM((TURNS, 2, ROWS, 128), f32),
           pltpu.VMEM((CH, 384), f32),
           pltpu.VMEM((288, 384), f32),
           pltpu.VMEM((288, 384), f32),
           pltpu.VMEM((2 * CH, 864), bf16),
           pltpu.VMEM((288, 912), bf16),
           pltpu.VMEM((1152, 768), bf16),
           pltpu.VMEM((2, CH, 384), f32),
           pltpu.VMEM((TILES + 2 * PADT, B + 2 * PADX, 128), f32),
           pltpu.VMEM((TURNS, TILES, B, 128), f32),
           pltpu.VMEM((912, 768), bf16),
           pltpu.VMEM((2 * TURNS * CH, 1152), bf16),
           pltpu.VMEM((2 * TURNS * CH, 768), f32),
           pltpu.VMEM((2 * CH, 768), f32),
           pltpu.VMEM((FRAG, FRAG, 8, 128), f32),
           pltpu.VMEM((FRAG, 128), f32),
           pltpu.VMEM((GRP, FRAG, 128), f32),
           dma((11,)), per_peer, per_peer, per_chunk, per_chunk, per_chunk, per_chunk, per_chunk,
           dma((2, CHUNKS, GRP)), dma((2, CHUNKS, GRP)), dma((2, CHUNKS, GRP)), dma((2, CHUNKS, GRP)),
           per_chunk, per_chunk, per_chunk, per_chunk, dma((GRP,)), dma((GRP,))],
        compiler_params=pltpu.CompilerParams(collective_id=0, has_side_effects=True, vmem_limit_bytes=48 << 20),
        name="exchange",
    )(orbitals, kernel, left, inverse, right, twiddle, anchors, count, first, second, reach)


def project_kernel(phi_ref, action_ref, total_ref, gradient_ref, lagrange_ref, flat):
    total = total_ref[...][:, 0:FRAG]
    lagrange = 0.5 * (total + total.T)
    lagrange_ref[0] = lagrange
    for a in range(FRAG):
        value = action_ref[a]
        for b in range(FRAG):
            value = value - lagrange[b:b + 1, a:a + 1] * phi_ref[b]
        flat[SLAB * a:SLAB * a + SLAB, :] = value
    for x in range(12):
        for t in range(TILES):
            gradient_ref[FRAG * x:FRAG * x + FRAG, 128 * t:128 * t + 128] = flat[pl.ds(TILES * x + t, FRAG, stride=SLAB), :]


def projected(phi, action, total):
    vmem = pl.BlockSpec(memory_space=pltpu.VMEM)
    return pl.pallas_call(
        project_kernel,
        out_shape=(jax.ShapeDtypeStruct((12 * FRAG, B * B), jnp.float32),
                   jax.ShapeDtypeStruct((1, FRAG, FRAG), jnp.float32)),
        in_specs=[vmem] * 3,
        out_specs=(vmem, vmem),
        scratch_shapes=[pltpu.VMEM((FRAG * SLAB, 128), jnp.float32)],
        compiler_params=pltpu.CompilerParams(vmem_limit_bytes=8 << 20),
        name="projected",
    )(phi, action, total)


def shards(orbitals, kernel, anchors, pair_count, pair_first, pair_second, pair_reach):
    phi, action, total = exchange(orbitals, kernel, anchors.T, pair_count, pair_first, pair_second, pair_reach)
    gradient, lagrange = projected(phi, action, total)
    return gradient.reshape(12, FRAG, B * B).transpose(1, 0, 2), lagrange


def solution(mesh):
    placed = (P(("orb", "grp"), None, None), P(), P(), P("orb"), P("orb"), P("orb"), P("orb"))
    return jax.shard_map(
        shards,
        mesh=mesh,
        in_specs=placed,
        out_specs=(P("orb", "grp", None), P("orb", None, None)),
        check_vma=False,
    )
```

```python
import functools
import math

import jax
import jax.numpy as jnp
import ml_dtypes
import numpy as np
from jax import lax
from jax.experimental import pallas as pl
from jax.experimental.pallas import tpu as pltpu
from jax.sharding import PartitionSpec as P

MESH = pl.DeviceIdType.MESH
B = 48
FRAG = 8
GRP = 4
TURNS = 2
TILES = 18
SLAB = 216
ROWS = 864
HALF = 25
CH = 152
PADX = 16
PADT = 8
CHUNKS = 9
CHUNK = SLAB // CHUNKS


def split(a):
    a = a.astype(np.float32)
    head = a.astype(ml_dtypes.bfloat16)
    tail = (a - head.astype(np.float32)).astype(ml_dtypes.bfloat16)
    return head, tail


@functools.lru_cache(None)
def tables():
    c, kx = np.meshgrid(np.arange(6), np.arange(HALF), indexing="ij")
    c, kx = c.reshape(-1, 1), kx.reshape(-1, 1)
    a, x = np.meshgrid(np.arange(6), np.arange(B), indexing="ij")
    a, x = a.reshape(1, -1), x.reshape(1, -1)
    theta = 2 * np.pi * ((8 * c * a + kx * x) % 48) / 48
    left = np.zeros((2 * CH, 288))
    left[:150] = np.cos(theta)
    left[CH:CH + 150] = -np.sin(theta)
    left = np.concatenate(split(left), axis=1)
    inverse = np.concatenate([left[:, :288].T, left[:, 288:].T], axis=1)
    b, z = np.meshgrid(np.arange(8), np.arange(B), indexing="ij")
    b, z = b.reshape(-1), z.reshape(-1)
    phi = 2 * np.pi * ((6 * np.outer(b, b) + np.outer(z, z)) % 48) / 48
    right = np.concatenate(split(np.concatenate([np.cos(phi), -np.sin(phi)], axis=1)), axis=0)
    turn = 2 * np.pi * ((np.arange(6)[:, None] * b[None, :]) % 48) / 48
    twiddle = np.stack([np.cos(turn), -np.sin(turn)]).astype(np.float32)
    return left, inverse, right, twiddle


def halves(value):
    head = value.astype(jnp.bfloat16)
    return head, (value - head.astype(jnp.float32)).astype(jnp.bfloat16)


def dot(a, b):
    return jnp.dot(a, b, preferred_element_type=jnp.float32)


def modes_of(kernel_ref, modes_ref, picked, mirrored):
    for c in range(6):
        for e in range(8):
            picked[48 * c:48 * c + 48, 48 * e:48 * e + 48] = kernel_ref[:, 48 * (c + 6 * e):48 * (c + 6 * e) + 48]
    lane = lax.broadcasted_iota(jnp.int32, (1, 384), 1)
    e, kz = lane // B, lane % B
    row = lax.broadcasted_iota(jnp.int32, (384, 384), 0)
    for shift, rows in ((0, slice(0, 48)), (1, slice(48, 288))):
        source = (16 - e - shift) % 8 * B + (B - kz) % B
        permute = jnp.where(row == source, 1.0, 0.0).astype(jnp.bfloat16)
        head, tail = halves(picked[rows, :])
        mirrored[rows, :] = dot(head, permute) + dot(tail, permute)
    out = lax.broadcasted_iota(jnp.int32, (32, B), 0)
    permute = jnp.where(lax.broadcasted_iota(jnp.int32, (32, B), 1) == (B - out) % B, 1.0, 0.0).astype(jnp.bfloat16)
    kx = lax.broadcasted_iota(jnp.int32, (32, 384), 0)
    weight = jnp.where((kx == 0) | (kx == HALF - 1), 0.5 / B**3, 1.0 / B**3)
    modes_ref[144:CH, :] = jnp.zeros((8, 384), jnp.float32)
    for c in range(6):
        other = (6 - c) % 6
        head, tail = halves(mirrored[48 * other:48 * other + 48, :])
        even = (picked[48 * c:48 * c + 32, :] + dot(permute, head) + dot(permute, tail)) * weight
        modes_ref[HALF * c:HALF * c + HALF, :] = even[:HALF]


def shifted(source, offset, emit):
    d0, d1, d2 = offset
    flat = 48 * d1 + d2 + 1024
    tile = lax.shift_right_logical(flat, 7) - 8
    lane_by = lax.bitwise_and(flat, 127)
    lane = lax.broadcasted_iota(jnp.int32, (B, 128), 1)
    late = lane >= lane_by
    insides = []
    for k in range(3):
        z = lax.rem(lane + 128 * k, B) - d2
        insides.append((z >= 0) & (z < B))
    before = None
    for t in range(-1, TILES):
        block = source[t - tile + PADT, pl.ds(PADX - d0, B), :]
        block = pltpu.roll(block, lane_by, 1)
        if t >= 0:
            emit(t, jnp.where(insides[t % 3], jnp.where(late, block, before), 0.0))
        before = block


def stack_tables(left_ref, inverse_ref, right_ref, twiddle_ref, left, inverse, right, twiddle):
    left[:, 0:288] = left_ref[:, 0:288]
    left[:, 288:864] = left_ref[...]
    inverse[:, 0:304] = inverse_ref[:, 0:304]
    inverse[:, 304:912] = inverse_ref[...]
    right[0:384, :] = right_ref[0:384, :]
    right[384:1152, :] = right_ref[...]
    for c in range(6):
        rows = slice(HALF * c, HALF * c + HALF + 2 * (c == 5))
        for part in range(2):
            twiddle[part, rows, :] = jnp.broadcast_to(twiddle_ref[part, c:c + 1, :], (rows.stop - rows.start, 384))


def block_of(t):
    return slice(48 * (t // 3), 48 * (t // 3) + 48), slice(128 * (t % 3), 128 * (t % 3) + 128)


def potentials(pairs, offsets, modes, left, inverse, right, twiddle, padded, moved, stack, wide, spec, volume):
    for turn in range(TURNS):
        for t in range(TILES):
            padded[t + PADT, pl.ds(PADX, B), :] = pairs[turn, 1, pl.ds(t, B, stride=TILES), :]

        def emit(t, block):
            moved[turn, t] = block
            density = pairs[turn, 0, pl.ds(t, B, stride=TILES), :] * block
            head, tail = halves(density)
            rows, lanes = block_of(t)
            lanes = slice(384 * turn + lanes.start, 384 * turn + lanes.stop)
            stack[rows.start:rows.stop, lanes] = head
            stack[288 + rows.start:288 + rows.stop, lanes] = tail
            stack[576 + rows.start:576 + rows.stop, lanes] = head

        shifted(padded, offsets[turn], emit)

    volume[0:2 * CH, :] = dot(left[...], stack[0:864, :])
    tr, ti = twiddle[0], twiddle[1]

    def put(row, value):
        head, tail = halves(value)
        wide[row:row + CH, 0:384] = head
        wide[row:row + CH, 384:768] = tail
        wide[row:row + CH, 768:1152] = head

    for turn in range(TURNS):
        re = volume[0:CH, 384 * turn:384 * turn + 384]
        im = volume[CH:2 * CH, 384 * turn:384 * turn + 384]
        put(2 * CH * turn, re * tr - im * ti)
        put(2 * CH * turn + CH, re * ti + im * tr)
    spec[...] = dot(wide[...], right[...])
    table = modes[...]
    for turn in range(TURNS):
        row = 2 * CH * turn
        re = spec[row:row + CH, 0:384] - spec[row + CH:row + 2 * CH, 384:768]
        im = spec[row:row + CH, 384:768] + spec[row + CH:row + 2 * CH, 0:384]
        put(row, re * table)
        put(row + CH, im * table)
    spec[...] = dot(wide[...], right[...])
    for turn in range(TURNS):
        row = 2 * CH * turn
        re = spec[row:row + CH, 0:384] + spec[row + CH:row + 2 * CH, 384:768]
        im = spec[row + CH:row + 2 * CH, 0:384] - spec[row:row + CH, 384:768]
        lanes = slice(384 * turn, 384 * turn + 384)
        for part, value in enumerate((re * tr + im * ti, im * tr - re * ti)):
            head, tail = halves(value)
            stack[CH * part:CH * part + CH, lanes] = head
            stack[304 + CH * part:304 + CH * part + CH, lanes] = tail
            stack[608 + CH * part:608 + CH * part + CH, lanes] = head
    volume[0:288, :] = dot(inverse[...], stack[...])


def back_terms(turn, pairs, offset, volume, padded, terms):
    for t in range(TILES):
        rows, lanes = block_of(t)
        potential = volume[rows, 384 * turn + lanes.start:384 * turn + lanes.stop]
        padded[t + PADT, pl.ds(PADX, B), :] = potential * pairs[turn, 0, pl.ds(t, B, stride=TILES), :]

    def emit(t, block):
        terms[1, turn, pl.ds(t, B, stride=TILES), :] = block

    shifted(padded, [-d for d in offset], emit)


def forward_terms(turn, volume, moved, terms):
    for t in range(TILES):
        rows, lanes = block_of(t)
        potential = volume[rows, 384 * turn + lanes.start:384 * turn + lanes.stop]
        terms[0, turn, pl.ds(t, B, stride=TILES), :] = potential * moved[turn, t]


def sibling(orb):
    return orb + 1 - 2 * lax.rem(orb, 2)


def exchange_kernel(orbitals, kernel, left_hbm, inverse_hbm, right_hbm, twiddle_hbm, anchors_hbm, count_hbm, first_hbm,
                    second_hbm, reach_hbm, gradient_ref, lagrange_ref, *scratch):
    scratch = list(scratch)

    def take(n):
        taken, scratch[:] = scratch[:n], scratch[n:]
        return taken

    near = take(3 * CHUNKS)
    out = take(2 * CHUNKS)
    landed, landed_back, aside, beside, onward, behind = (take(CHUNKS) for _ in range(6))
    landed = (landed, landed_back)
    native, kernel_ref, left_ref, inverse_ref, right_ref, twiddle_ref = take(6)
    anchors, count, first, second, reach, weights = take(6)
    mine, pairs, terms, modes, picked, mirrored, left, inverse, right, twiddle = take(10)
    padded, moved, stack, wide, spec, volume = take(6)
    products, block, blocks, phi, action, flat = take(6)
    (load_sem, send_slab, recv_slab, own_sem, send_ahead, recv_ahead, send_side, recv_side, send_pick, recv_pick,
     send_term, recv_term, send_back, recv_back, send_on, recv_on, send_sum, recv_sum) = scratch
    orb, me = lax.axis_index("orb"), lax.axis_index("grp")
    orbs = lax.axis_size("orb")
    even = lax.rem(orb, 2) == 0
    is_even = jnp.where(even, 1.0, 0.0)
    sources = (orbitals, first_hbm, second_hbm, reach_hbm, kernel, left_hbm, inverse_hbm, right_hbm, twiddle_hbm,
               anchors_hbm, count_hbm)
    places = (native, first, second, reach, kernel_ref, left_ref, inverse_ref, right_ref, twiddle_ref, anchors, count)
    loads = [pltpu.make_async_copy(s, p, load_sem.at[i]) for i, (s, p) in enumerate(zip(sources, places))]
    for load in loads:
        load.start()
    barrier = pltpu.get_barrier_semaphore()
    for step in range(1, GRP):
        pl.semaphore_signal(barrier, inc=1, device_id={"grp": lax.rem(me + step, GRP)}, device_id_type=MESH)
    for other in (sibling(orb), lax.rem(orb + 2, orbs), lax.rem(orb + orbs - 2, orbs)):
        pl.semaphore_signal(barrier, inc=1, device_id={"orb": other}, device_id_type=MESH)
    loads[0].wait()
    for j in range(2):
        for t in range(TILES):
            mine[j, pl.ds(t, B, stride=TILES), :] = native[j, :, 128 * t:128 * t + 128]
    pl.semaphore_wait(barrier, GRP - 1 + 3)

    def rows(c):
        return pl.ds(CHUNK * c, CHUNK)

    def peers():
        return [(step, lax.rem(me + step, GRP)) for step in (2, 1, 3)]

    def at_slab(member, c):
        return pl.ds(pl.multiple_of(SLAB * member + CHUNK * c, 8), CHUNK)

    slabs, owns = [], []
    for c in range(CHUNKS):
        slabs.append([pltpu.make_async_remote_copy(
            src_ref=mine.at[:, at_slab(other, c)], dst_ref=near[3 * c].at[pl.ds(2 * me, 2)],
            send_sem=send_slab.at[c, step], recv_sem=recv_slab.at[c, step],
            device_id={"grp": other}, device_id_type=MESH) for step, other in peers()])
        owns.append(pltpu.make_async_copy(mine.at[:, at_slab(me, c)], near[3 * c].at[pl.ds(2 * me, 2)], own_sem.at[c]))
        owns[c].start()
        for copy in slabs[c]:
            copy.start()

    ahead = [pltpu.make_async_remote_copy(
        src_ref=near[3 * c], dst_ref=near[3 * c + 2], send_sem=send_ahead.at[c], recv_sem=recv_ahead.at[c],
        device_id={"orb": lax.rem(orb + orbs - 2, orbs)}, device_id_type=MESH) for c in range(CHUNKS)]
    side = [[pltpu.make_async_remote_copy(
        src_ref=near[3 * c + which], dst_ref=near[3 * c + 1], send_sem=send_side.at[c], recv_sem=recv_side.at[c],
        device_id={"orb": sibling(orb)}, device_id_type=MESH) for which in (2, 0)] for c in range(CHUNKS)]
    picks = [[[pltpu.make_async_remote_copy(
        src_ref=out[2 * c + which].at[other], dst_ref=pairs.at[:, which, at_slab(me, c)],
        send_sem=send_pick.at[which, c, step], recv_sem=recv_pick.at[which, c, step],
        device_id={"grp": other}, device_id_type=MESH) for step, other in peers()]
        for c in range(CHUNKS)] for which in range(2)]

    def choose(which, c):
        for slot in range(GRP * TURNS):
            if which == 0:
                value = near[3 * c][first[slot]]
            else:
                value = near[3 * c][second[slot]]
                value = jnp.where(reach[slot] == 1, near[3 * c + 1][second[slot]], value)
                value = jnp.where(reach[slot] == 2, near[3 * c + 2][second[slot]], value)
            out[2 * c + which][slot % GRP, slot // GRP] = value
        for copy in picks[which][c]:
            copy.start()
        pairs[:, which, at_slab(me, c), :] = out[2 * c + which][me]

    for load in loads[1:4]:
        load.wait()
    for c in range(CHUNKS):
        owns[c].wait()
        for copy in slabs[c]:
            copy.wait_recv()
        ahead[c].start()

        @pl.when(jnp.logical_not(even))
        def _():
            side[c][1].start()

        choose(0, c)
        phi[:, CHUNK * c:CHUNK * c + CHUNK, :] = near[3 * c][...]
        if c == 0:
            for load in loads[4:]:
                load.wait()
            stack_tables(left_ref, inverse_ref, right_ref, twiddle_ref, left, inverse, right, twiddle)
        if c == 1:
            modes_of(kernel_ref, modes, picked, mirrored)
        if c == 2:
            padded[...] = jnp.zeros_like(padded)
        if c == 3:
            for slot in range(GRP * TURNS):
                live = jnp.where(slot < count[0], 1.0, 0.0)
                for a in range(FRAG):
                    weights[0, FRAG * slot + a] = jnp.where(first[slot] == a, live, 0.0)
                    hit = jnp.where(second[slot] == a, live, 0.0)
                    for far in range(3):
                        weights[1 + far, FRAG * slot + a] = jnp.where(reach[slot] == far, hit, 0.0)
    for c in range(CHUNKS + 1):
        if c < CHUNKS:
            ahead[c].wait_recv()

            @pl.when(even)
            def _():
                side[c][0].start()

        if c > 0:
            side[c - 1][0].wait_recv()
            choose(1, c - 1)
    for c in range(CHUNKS):
        for which in range(2):
            for copy in picks[which][c]:
                copy.wait_recv()

    offsets = []
    for turn in range(TURNS):
        far = reach[me + GRP * turn]
        offsets.append([anchors[k, lax.rem(orb + far, orbs)] - anchors[k, orb] for k in range(3)])
    potentials(pairs, offsets, modes, left, inverse, right, twiddle, padded, moved, stack, wide, spec, volume)

    sends = [[[pltpu.make_async_remote_copy(
        src_ref=terms.at[which, :, at_slab(other, c)], dst_ref=landed[which][c].at[me],
        send_sem=send_term.at[which, c, step], recv_sem=recv_term.at[which, c, step],
        device_id={"grp": other}, device_id_type=MESH) for step, other in peers()]
        for c in range(CHUNKS)] for which in range(2)]
    for turn in range(TURNS):
        back_terms(turn, pairs, offsets[turn], volume, padded, terms)
    for c in range(CHUNKS):
        for copy in sends[1][c]:
            copy.start()
    for turn in range(TURNS):
        forward_terms(turn, volume, moved, terms)
    for c in range(CHUNKS):
        for copy in sends[0][c]:
            copy.start()
    back = [pltpu.make_async_remote_copy(
        src_ref=aside[c], dst_ref=beside[c], send_sem=send_back.at[c], recv_sem=recv_back.at[c],
        device_id={"orb": sibling(orb)}, device_id_type=MESH) for c in range(CHUNKS)]
    on = [pltpu.make_async_remote_copy(
        src_ref=onward[c], dst_ref=behind[c], send_sem=send_on.at[c], recv_sem=recv_on.at[c],
        device_id={"orb": lax.rem(orb + 2, orbs)}, device_id_type=MESH) for c in range(CHUNKS)]

    def summed(c, a, kind):
        value = jnp.zeros((CHUNK, 128), jnp.float32)
        for slot in range(GRP * TURNS):
            term = landed[kind > 0][c][slot % GRP, slot // GRP]
            value = value + weights[kind, FRAG * slot + a] * term
        return value

    for c in range(CHUNKS):
        landed[1][c][me] = terms[1, :, at_slab(me, c), :]
    for c in range(CHUNKS):
        for copy in sends[1][c]:
            copy.wait_recv()
        for a in range(FRAG):
            aside[c][a] = summed(c, a, 2)
        back[c].start()
        for a in range(FRAG):
            onward[c][a] = summed(c, a, 3)
        back[c].wait_recv()
        for a in range(FRAG):
            onward[c][a] = onward[c][a] + is_even * beside[c][a]
        on[c].start()
        for a in range(FRAG):
            action[a, CHUNK * c:CHUNK * c + CHUNK, :] = summed(c, a, 1) + (1.0 - is_even) * beside[c][a]
        landed[0][c][me] = terms[0, :, at_slab(me, c), :]
    products[...] = jnp.zeros_like(products)
    for c in range(CHUNKS):
        for copy in sends[0][c]:
            copy.wait_recv()
        for b in range(FRAG):
            action[b, CHUNK * c:CHUNK * c + CHUNK, :] += summed(c, b, 0)
        on[c].wait_recv()
        for b in range(FRAG):
            value = action[b, CHUNK * c:CHUNK * c + CHUNK, :] + behind[c][b]
            action[b, CHUNK * c:CHUNK * c + CHUNK, :] = value
            for a in range(FRAG):
                part = jnp.sum((phi[a, CHUNK * c:CHUNK * c + CHUNK, :] * value).reshape(CHUNK // 8, 8, 128), axis=0)
                products[b, a] = products[b, a] + part
    lane = lax.broadcasted_iota(jnp.int32, (FRAG, 128), 1)
    total = jnp.zeros((FRAG, 128), jnp.float32)
    for b in range(FRAG):
        part = jnp.sum(jnp.sum(products[b], axis=1), axis=1, keepdims=True)
        total = total + jnp.where(lane == b, part, 0.0)
    block[...] = total
    sums = []
    for step, other in peers():
        sums.append(pltpu.make_async_remote_copy(
            src_ref=block, dst_ref=blocks.at[step], send_sem=send_sum.at[step], recv_sem=recv_sum.at[step],
            device_id={"grp": other}, device_id_type=MESH))
        sums[-1].start()
    for c in range(CHUNKS):
        for copy in slabs[c] + [ahead[c], back[c], on[c]] + [k for w in range(2) for k in picks[w][c] + sends[w][c]]:
            copy.wait_send()

        @pl.when(even)
        def _():
            side[c][0].wait_send()

        @pl.when(jnp.logical_not(even))
        def _():
            side[c][1].wait_send()

    for copy in sums:
        copy.wait()
    total = (((block[...] + blocks[2]) + (blocks[1] + blocks[3])) / float(B**3))[:, 0:FRAG]
    lagrange = 0.5 * (total + total.T)
    lagrange_ref[0] = lagrange
    for a in range(FRAG):
        value = action[a]
        for b in range(FRAG):
            value = value - lagrange[b:b + 1, a:a + 1] * phi[b]
        flat[SLAB * a:SLAB * a + SLAB, :] = value
    for x in range(12):
        for t in range(TILES):
            gradient_ref[FRAG * x:FRAG * x + FRAG, 128 * t:128 * t + 128] = flat[pl.ds(TILES * x + t, FRAG, stride=SLAB), :]


def exchange(orbitals, kernel, anchors, count, first, second, reach):
    left, inverse, right, twiddle = (jnp.asarray(t) for t in tables())
    vmem, hbm = pl.BlockSpec(memory_space=pltpu.VMEM), pl.BlockSpec(memory_space=pltpu.HBM)
    dma, f32, bf16 = pltpu.SemaphoreType.DMA, jnp.float32, jnp.bfloat16
    per_chunk, per_peer = dma((CHUNKS,)), dma((CHUNKS, GRP))
    part = pltpu.VMEM((FRAG, CHUNK, 128), f32)
    return pl.pallas_call(
        exchange_kernel,
        out_shape=(jax.ShapeDtypeStruct((12 * FRAG, B * B), f32), jax.ShapeDtypeStruct((1, FRAG, FRAG), f32)),
        in_specs=[hbm] * 11,
        out_specs=(vmem, vmem),
        scratch_shapes=[part] * (3 * CHUNKS)
        + [pltpu.VMEM((GRP, TURNS, CHUNK, 128), f32)] * (2 * CHUNKS)
        + [pltpu.VMEM((GRP, TURNS, CHUNK, 128), f32)] * (2 * CHUNKS)
        + [part] * (4 * CHUNKS)
        + [pltpu.VMEM(a.shape, a.dtype) for a in (orbitals, kernel, left, inverse, right, twiddle)]
        + [pltpu.SMEM(a.shape, a.dtype) for a in (anchors, count, first, second, reach)]
        + [pltpu.SMEM((4, FRAG * GRP * TURNS), f32)]
        + [pltpu.VMEM((2, ROWS, 128), f32),
           pltpu.VMEM((TURNS, 2, ROWS, 128), f32),
           pltpu.VMEM((TURNS, 2, ROWS, 128), f32),
           pltpu.VMEM((CH, 384), f32),
           pltpu.VMEM((288, 384), f32),
           pltpu.VMEM((288, 384), f32),
           pltpu.VMEM((2 * CH, 864), bf16),
           pltpu.VMEM((288, 912), bf16),
           pltpu.VMEM((1152, 768), bf16),
           pltpu.VMEM((2, CH, 384), f32),
           pltpu.VMEM((TILES + 2 * PADT, B + 2 * PADX, 128), f32),
           pltpu.VMEM((TURNS, TILES, B, 128), f32),
           pltpu.VMEM((912, 768), bf16),
           pltpu.VMEM((2 * TURNS * CH, 1152), bf16),
           pltpu.VMEM((2 * TURNS * CH, 768), f32),
           pltpu.VMEM((2 * CH, 768), f32),
           pltpu.VMEM((FRAG, FRAG, 8, 128), f32),
           pltpu.VMEM((FRAG, 128), f32),
           pltpu.VMEM((GRP, FRAG, 128), f32),
           pltpu.VMEM((FRAG, SLAB, 128), f32),
           pltpu.VMEM((FRAG, SLAB, 128), f32),
           pltpu.VMEM((FRAG * SLAB, 128), f32),
           dma((11,)), per_peer, per_peer, per_chunk, per_chunk, per_chunk, per_chunk, per_chunk,
           dma((2, CHUNKS, GRP)), dma((2, CHUNKS, GRP)), dma((2, CHUNKS, GRP)), dma((2, CHUNKS, GRP)),
           per_chunk, per_chunk, per_chunk, per_chunk, dma((GRP,)), dma((GRP,))],
        compiler_params=pltpu.CompilerParams(collective_id=0, has_side_effects=True, vmem_limit_bytes=67043328),
        name="exchange",
    )(orbitals, kernel, left, inverse, right, twiddle, anchors, count, first, second, reach)


def shards(orbitals, kernel, anchors, pair_count, pair_first, pair_second, pair_reach):
    gradient, lagrange = exchange(orbitals, kernel, anchors.T, pair_count, pair_first, pair_second, pair_reach)
    return gradient.reshape(12, FRAG, B * B).transpose(1, 0, 2), lagrange


def solution(mesh):
    placed = (P(("orb", "grp"), None, None), P(), P(), P("orb"), P("orb"), P("orb"), P("orb"))
    return jax.shard_map(
        shards,
        mesh=mesh,
        in_specs=placed,
        out_specs=(P("orb", "grp", None), P("orb", None, None)),
        check_vma=False,
    )
```

```python
import functools
import math

import jax
import jax.numpy as jnp
import ml_dtypes
import numpy as np
from jax import lax
from jax.experimental import pallas as pl
from jax.experimental.pallas import tpu as pltpu
from jax.sharding import PartitionSpec as P

MESH = pl.DeviceIdType.MESH
B = 48
FRAG = 8
GRP = 4
TURNS = 2
TILES = 18
SLAB = 216
ROWS = 864
HALF = 25
CH = 152
PADX = 16
PADT = 8
BANDS = 3
AHEAD_Y = 9
AHEAD_Z = 4
PARTS = (24, 40, 40, 40, 40, 32)
CHUNKS = len(PARTS)
STARTS = tuple(sum(PARTS[:c]) for c in range(CHUNKS))


def split(a):
    a = a.astype(np.float32)
    head = a.astype(ml_dtypes.bfloat16)
    tail = (a - head.astype(np.float32)).astype(ml_dtypes.bfloat16)
    return head, tail


@functools.lru_cache(None)
def tables():
    c, kx = np.meshgrid(np.arange(6), np.arange(HALF), indexing="ij")
    c, kx = c.reshape(-1, 1), kx.reshape(-1, 1)
    a, x = np.meshgrid(np.arange(6), np.arange(B), indexing="ij")
    a, x = a.reshape(1, -1), x.reshape(1, -1)
    theta = 2 * np.pi * ((8 * c * a + kx * x) % 48) / 48
    left = np.zeros((2 * CH, 288))
    left[:150] = np.cos(theta)
    left[CH:CH + 150] = -np.sin(theta)
    left = np.concatenate(split(left), axis=1)
    inverse = np.concatenate([left[:, :288].T, left[:, 288:].T], axis=1)
    b, z = np.meshgrid(np.arange(8), np.arange(B), indexing="ij")
    b, z = b.reshape(-1), z.reshape(-1)
    phi = 2 * np.pi * ((6 * np.outer(b, b) + np.outer(z, z)) % 48) / 48
    right = np.concatenate(split(np.concatenate([np.cos(phi), -np.sin(phi)], axis=1)), axis=0)
    turn = 2 * np.pi * ((np.arange(6)[:, None] * b[None, :]) % 48) / 48
    twiddle = np.stack([np.cos(turn), -np.sin(turn)]).astype(np.float32)
    return left, inverse, right, twiddle


def halves(value):
    head = value.astype(jnp.bfloat16)
    return head, (value - head.astype(jnp.float32)).astype(jnp.bfloat16)


def dot(a, b):
    return jnp.dot(a, b, preferred_element_type=jnp.float32)


def modes_of(kernel_ref, modes_ref, picked, mirrored):
    for c in range(6):
        for e in range(8):
            picked[48 * c:48 * c + 48, 48 * e:48 * e + 48] = kernel_ref[:, 48 * (c + 6 * e):48 * (c + 6 * e) + 48]
    lane = lax.broadcasted_iota(jnp.int32, (1, 384), 1)
    e, kz = lane // B, lane % B
    row = lax.broadcasted_iota(jnp.int32, (384, 384), 0)
    for shift, rows in ((0, slice(0, 48)), (1, slice(48, 288))):
        source = (16 - e - shift) % 8 * B + (B - kz) % B
        permute = jnp.where(row == source, 1.0, 0.0).astype(jnp.bfloat16)
        head, tail = halves(picked[rows, :])
        mirrored[rows, :] = dot(head, permute) + dot(tail, permute)
    out = lax.broadcasted_iota(jnp.int32, (32, B), 0)
    permute = jnp.where(lax.broadcasted_iota(jnp.int32, (32, B), 1) == (B - out) % B, 1.0, 0.0).astype(jnp.bfloat16)
    kx = lax.broadcasted_iota(jnp.int32, (32, 384), 0)
    weight = jnp.where((kx == 0) | (kx == HALF - 1), 0.5 / B**3, 1.0 / B**3)
    modes_ref[144:CH, :] = jnp.zeros((8, 384), jnp.float32)
    for c in range(6):
        other = (6 - c) % 6
        head, tail = halves(mirrored[48 * other:48 * other + 48, :])
        even = (picked[48 * c:48 * c + 32, :] + dot(permute, head) + dot(permute, tail)) * weight
        modes_ref[HALF * c:HALF * c + HALF, :] = even[:HALF]


def shifted(source, offset, emit):
    d0, d1, d2 = offset
    flat = 48 * d1 + d2 + 1024
    tile = lax.shift_right_logical(flat, 7) - 8
    lane_by = lax.bitwise_and(flat, 127)
    lane = lax.broadcasted_iota(jnp.int32, (B, 128), 1)
    late = lane >= lane_by
    insides = []
    for k in range(3):
        z = lax.rem(lane + 128 * k, B) - d2
        insides.append((z >= 0) & (z < B))
    before = None
    for t in range(-1, TILES):
        block = source[t - tile + PADT, pl.ds(PADX - d0, B), :]
        block = pltpu.roll(block, lane_by, 1)
        if t >= 0:
            emit(t, jnp.where(insides[t % 3], jnp.where(late, block, before), 0.0))
        before = block


def stack_tables(left_ref, inverse_ref, right_ref, twiddle_ref, left, inverse, right, twiddle):
    left[:, 0:288] = left_ref[:, 0:288]
    left[:, 288:864] = left_ref[...]
    inverse[:, 0:304] = inverse_ref[:, 0:304]
    inverse[:, 304:912] = inverse_ref[...]
    right[0:384, :] = right_ref[0:384, :]
    right[384:1152, :] = right_ref[...]
    for c in range(6):
        rows = slice(HALF * c, HALF * c + HALF + 2 * (c == 5))
        for part in range(2):
            twiddle[part, rows, :] = jnp.broadcast_to(twiddle_ref[part, c:c + 1, :], (rows.stop - rows.start, 384))


def block_of(t):
    return slice(48 * (t // 3), 48 * (t // 3) + 48), slice(128 * (t % 3), 128 * (t % 3) + 128)


def potentials(pairs, offsets, modes, left, inverse, right, twiddle, padded, moved, stack, wide, spec, volume):
    for turn in range(TURNS):
        for t in range(TILES):
            padded[t + PADT, pl.ds(PADX, B), :] = pairs[turn, 1, pl.ds(t, B, stride=TILES), :]

        def emit(t, block):
            moved[turn, t] = block
            density = pairs[turn, 0, pl.ds(t, B, stride=TILES), :] * block
            head, tail = halves(density)
            rows, lanes = block_of(t)
            lanes = slice(384 * turn + lanes.start, 384 * turn + lanes.stop)
            stack[rows.start:rows.stop, lanes] = head
            stack[288 + rows.start:288 + rows.stop, lanes] = tail
            stack[576 + rows.start:576 + rows.stop, lanes] = head

        shifted(padded, offsets[turn], emit)

    volume[0:2 * CH, :] = dot(left[...], stack[0:864, :])
    tr, ti = twiddle[0], twiddle[1]

    def put(row, value):
        head, tail = halves(value)
        wide[row:row + CH, 0:384] = head
        wide[row:row + CH, 384:768] = tail
        wide[row:row + CH, 768:1152] = head

    for turn in range(TURNS):
        re = volume[0:CH, 384 * turn:384 * turn + 384]
        im = volume[CH:2 * CH, 384 * turn:384 * turn + 384]
        put(2 * CH * turn, re * tr - im * ti)
        put(2 * CH * turn + CH, re * ti + im * tr)
    spec[...] = dot(wide[...], right[...])
    table = modes[...]
    for turn in range(TURNS):
        row = 2 * CH * turn
        re = spec[row:row + CH, 0:384] - spec[row + CH:row + 2 * CH, 384:768]
        im = spec[row:row + CH, 384:768] + spec[row + CH:row + 2 * CH, 0:384]
        put(row, re * table)
        put(row + CH, im * table)
    spec[...] = dot(wide[...], right[...])
    for turn in range(TURNS):
        row = 2 * CH * turn
        re = spec[row:row + CH, 0:384] + spec[row + CH:row + 2 * CH, 384:768]
        im = spec[row + CH:row + 2 * CH, 0:384] - spec[row:row + CH, 384:768]
        lanes = slice(384 * turn, 384 * turn + 384)
        for part, value in enumerate((re * tr + im * ti, im * tr - re * ti)):
            head, tail = halves(value)
            stack[CH * part:CH * part + CH, lanes] = head
            stack[304 + CH * part:304 + CH * part + CH, lanes] = tail
            stack[608 + CH * part:608 + CH * part + CH, lanes] = head
    volume[0:288, :] = dot(inverse[...], stack[...])


def back_terms(turn, pairs, offset, volume, padded, terms):
    for t in range(TILES):
        rows, lanes = block_of(t)
        potential = volume[rows, 384 * turn + lanes.start:384 * turn + lanes.stop]
        padded[t + PADT, pl.ds(PADX, B), :] = potential * pairs[turn, 0, pl.ds(t, B, stride=TILES), :]

    def emit(t, block):
        terms[1, turn, pl.ds(t, B, stride=TILES), :] = block

    shifted(padded, [-d for d in offset], emit)


def forward_terms(turn, volume, moved, terms):
    for t in range(TILES):
        rows, lanes = block_of(t)
        potential = volume[rows, 384 * turn + lanes.start:384 * turn + lanes.stop]
        terms[0, turn, pl.ds(t, B, stride=TILES), :] = potential * moved[turn, t]


def sibling(orb):
    return orb + 1 - 2 * lax.rem(orb, 2)


def exchange_kernel(orbitals, kernel, left_hbm, inverse_hbm, right_hbm, twiddle_hbm, anchors_hbm, count_hbm, first_hbm,
                    second_hbm, reach_hbm, phi_hbm, action_hbm, total_ref, *scratch):
    scratch = list(scratch)

    def take(n):
        taken, scratch[:] = scratch[:n], scratch[n:]
        return taken

    near = take(3 * CHUNKS)
    out = take(2 * CHUNKS)
    landed, landed_back, aside, beside, onward, behind = (take(CHUNKS) for _ in range(6))
    landed = (landed, landed_back)
    native, kernel_ref, left_ref, inverse_ref, right_ref, twiddle_ref = take(6)
    anchors, count, first, second, reach, weights = take(6)
    mine, pairs, terms, modes, picked, mirrored, left, inverse, right, twiddle = take(10)
    padded, moved, stack, wide, spec, volume = take(6)
    products, block, blocks, action, phi_rows, action_rows = take(6)
    (load_sem, send_slab, recv_slab, own_sem, send_ahead, recv_ahead, send_side, recv_side, send_pick, recv_pick,
     send_term, recv_term, out_sem, send_back, recv_back, send_on, recv_on, send_sum, recv_sum) = scratch
    orb, me = lax.axis_index("orb"), lax.axis_index("grp")
    orbs = lax.axis_size("orb")
    even = lax.rem(orb, 2) == 0
    is_even = jnp.where(even, 1.0, 0.0)
    sources = (orbitals, first_hbm, second_hbm, reach_hbm, kernel, left_hbm, inverse_hbm, right_hbm, twiddle_hbm,
               anchors_hbm, count_hbm)
    places = (native, first, second, reach, kernel_ref, left_ref, inverse_ref, right_ref, twiddle_ref, anchors, count)
    loads = [pltpu.make_async_copy(s, p, load_sem.at[i]) for i, (s, p) in enumerate(zip(sources, places))]
    for load in loads:
        load.start()
    barrier = pltpu.get_barrier_semaphore()
    for step in range(1, GRP):
        pl.semaphore_signal(barrier, inc=1, device_id={"grp": lax.rem(me + step, GRP)}, device_id_type=MESH)
    for other in (sibling(orb), lax.rem(orb + 2, orbs), lax.rem(orb + orbs - 2, orbs)):
        pl.semaphore_signal(barrier, inc=1, device_id={"orb": other}, device_id_type=MESH)
    loads[0].wait()
    for j in range(2):
        for t in range(TILES):
            mine[j, pl.ds(t, B, stride=TILES), :] = native[j, :, 128 * t:128 * t + 128]
    pl.semaphore_wait(barrier, GRP - 1 + 3)

    def rows(c):
        return pl.ds(STARTS[c], PARTS[c])

    def peers():
        return [(step, lax.rem(me + step, GRP)) for step in (2, 1, 3)]

    def at_slab(member, c):
        return pl.ds(pl.multiple_of(SLAB * member + STARTS[c], 8), PARTS[c])

    slabs, owns = [], []
    for c in range(CHUNKS):
        slabs.append([pltpu.make_async_remote_copy(
            src_ref=mine.at[:, at_slab(other, c)], dst_ref=near[3 * c].at[pl.ds(2 * me, 2)],
            send_sem=send_slab.at[c, step], recv_sem=recv_slab.at[c, step],
            device_id={"grp": other}, device_id_type=MESH) for step, other in peers()])
        owns.append(pltpu.make_async_copy(mine.at[:, at_slab(me, c)], near[3 * c].at[pl.ds(2 * me, 2)], own_sem.at[c]))
        owns[c].start()
        if c < AHEAD_Y:
            for copy in slabs[c]:
                copy.start()

    ahead = [pltpu.make_async_remote_copy(
        src_ref=near[3 * c], dst_ref=near[3 * c + 2], send_sem=send_ahead.at[c], recv_sem=recv_ahead.at[c],
        device_id={"orb": lax.rem(orb + orbs - 2, orbs)}, device_id_type=MESH) for c in range(CHUNKS)]
    side = [[pltpu.make_async_remote_copy(
        src_ref=near[3 * c + which], dst_ref=near[3 * c + 1], send_sem=send_side.at[c], recv_sem=recv_side.at[c],
        device_id={"orb": sibling(orb)}, device_id_type=MESH) for which in (2, 0)] for c in range(CHUNKS)]
    picks = [[[pltpu.make_async_remote_copy(
        src_ref=out[2 * c + which].at[other], dst_ref=pairs.at[:, which, at_slab(me, c)],
        send_sem=send_pick.at[which, c, step], recv_sem=recv_pick.at[which, c, step],
        device_id={"grp": other}, device_id_type=MESH) for step, other in peers()]
        for c in range(CHUNKS)] for which in range(2)]

    bands = 3
    band = 12 * FRAG // bands
    phi_outs, action_outs = ([pltpu.make_async_copy(
        ref.at[pl.ds(band * k, band)], place.at[pl.ds(band * k, band)], out_sem.at[i, k]) for k in range(bands)]
        for i, (ref, place) in enumerate(((phi_rows, phi_hbm), (action_rows, action_hbm))))

    def lay(source, c, rows_ref, outs):
        for r in range(STARTS[c], STARTS[c] + PARTS[c]):
            x, t = r // TILES, r % TILES
            rows_ref[FRAG * x:FRAG * x + FRAG, 128 * t:128 * t + 128] = source(r)
            if (r + 1) % (SLAB // bands) == 0:
                outs[r // (SLAB // bands)].start()

    def choose(which, c):
        for slot in range(GRP * TURNS):
            if which == 0:
                value = near[3 * c][first[slot]]
            else:
                value = near[3 * c][second[slot]]
                value = jnp.where(reach[slot] == 1, near[3 * c + 1][second[slot]], value)
                value = jnp.where(reach[slot] == 2, near[3 * c + 2][second[slot]], value)
            out[2 * c + which][slot % GRP, slot // GRP] = value
        for copy in picks[which][c]:
            copy.start()
        pairs[:, which, at_slab(me, c), :] = out[2 * c + which][me]

    for load in loads[1:4]:
        load.wait()
    for tick in range(CHUNKS + AHEAD_Z + 1):
        c = tick
        if c < CHUNKS:
            owns[c].wait()
            for copy in slabs[c]:
                copy.wait_recv()
            ahead[c].start()

            @pl.when(jnp.logical_not(even))
            def _():
                side[c][1].start()

            if c + AHEAD_Y < CHUNKS:
                for copy in slabs[c + AHEAD_Y]:
                    copy.start()
            choose(0, c)
            lay(lambda r: near[3 * c][:, r - STARTS[c], :], c, phi_rows, phi_outs)
        if c == 0:
            for load in loads[4:]:
                load.wait()
            stack_tables(left_ref, inverse_ref, right_ref, twiddle_ref, left, inverse, right, twiddle)
        if c == 1:
            modes_of(kernel_ref, modes, picked, mirrored)
        if c == 2:
            padded[...] = jnp.zeros_like(padded)
        if c == 3:
            for slot in range(GRP * TURNS):
                live = jnp.where(slot < count[0], 1.0, 0.0)
                for a in range(FRAG):
                    weights[0, FRAG * slot + a] = jnp.where(first[slot] == a, live, 0.0)
                    hit = jnp.where(second[slot] == a, live, 0.0)
                    for far in range(3):
                        weights[1 + far, FRAG * slot + a] = jnp.where(reach[slot] == far, hit, 0.0)
        c = tick - AHEAD_Z
        if 0 <= c < CHUNKS:
            ahead[c].wait_recv()

            @pl.when(even)
            def _():
                side[c][0].start()

        c = tick - AHEAD_Z - 1
        if 0 <= c < CHUNKS:
            side[c][0].wait_recv()
            choose(1, c)
    for c in range(CHUNKS):
        for which in range(2):
            for copy in picks[which][c]:
                copy.wait_recv()

    offsets = []
    for turn in range(TURNS):
        far = reach[me + GRP * turn]
        offsets.append([anchors[k, lax.rem(orb + far, orbs)] - anchors[k, orb] for k in range(3)])
    potentials(pairs, offsets, modes, left, inverse, right, twiddle, padded, moved, stack, wide, spec, volume)

    sends = [[[pltpu.make_async_remote_copy(
        src_ref=terms.at[which, :, at_slab(other, c)], dst_ref=landed[which][c].at[me],
        send_sem=send_term.at[which, c, step], recv_sem=recv_term.at[which, c, step],
        device_id={"grp": other}, device_id_type=MESH) for step, other in peers()]
        for c in range(CHUNKS)] for which in range(2)]
    for turn in range(TURNS):
        back_terms(turn, pairs, offsets[turn], volume, padded, terms)
    for c in range(min(AHEAD_Y, CHUNKS)):
        for copy in sends[1][c]:
            copy.start()
    for turn in range(TURNS):
        forward_terms(turn, volume, moved, terms)
    back = [pltpu.make_async_remote_copy(
        src_ref=aside[c], dst_ref=beside[c], send_sem=send_back.at[c], recv_sem=recv_back.at[c],
        device_id={"orb": sibling(orb)}, device_id_type=MESH) for c in range(CHUNKS)]
    on = [pltpu.make_async_remote_copy(
        src_ref=onward[c], dst_ref=behind[c], send_sem=send_on.at[c], recv_sem=recv_on.at[c],
        device_id={"orb": lax.rem(orb + 2, orbs)}, device_id_type=MESH) for c in range(CHUNKS)]

    def summed(c, a, kind):
        value = jnp.zeros((PARTS[c], 128), jnp.float32)
        for slot in range(GRP * TURNS):
            term = landed[kind > 0][c][slot % GRP, slot // GRP]
            value = value + weights[kind, FRAG * slot + a] * term
        return value

    products[...] = jnp.zeros_like(products)
    for c in range(CHUNKS):
        landed[1][c][me] = terms[1, :, at_slab(me, c), :]
    for tick in range(CHUNKS + AHEAD_Z):
        c = tick
        if c < CHUNKS:
            for copy in sends[1][c]:
                copy.wait_recv()
            for copy in (sends[1][c + AHEAD_Y] if c + AHEAD_Y < CHUNKS else []):
                copy.start()
            for a in range(FRAG):
                aside[c][a] = summed(c, a, 2)
            back[c].start()
            for a in range(FRAG):
                onward[c][a] = summed(c, a, 3)
            back[c].wait_recv()
            for a in range(FRAG):
                onward[c][a] = onward[c][a] + is_even * beside[c][a]
            on[c].start()
            for copy in sends[0][c]:
                copy.start()
            for a in range(FRAG):
                action[a, STARTS[c]:STARTS[c] + PARTS[c], :] = summed(c, a, 1) + (1.0 - is_even) * beside[c][a]
            landed[0][c][me] = terms[0, :, at_slab(me, c), :]
        c = tick - AHEAD_Z
        if c >= 0:
            for copy in sends[0][c]:
                copy.wait_recv()
            for b in range(FRAG):
                action[b, STARTS[c]:STARTS[c] + PARTS[c], :] += summed(c, b, 0)
            on[c].wait_recv()
            for b in range(FRAG):
                value = action[b, STARTS[c]:STARTS[c] + PARTS[c], :] + behind[c][b]
                action[b, STARTS[c]:STARTS[c] + PARTS[c], :] = value
                for a in range(FRAG):
                    part = jnp.sum((near[3 * c][a] * value).reshape(PARTS[c] // 8, 8, 128), axis=0)
                    products[b, a] = products[b, a] + part
            lay(lambda r: action[:, r, :], c, action_rows, action_outs)
    lane = lax.broadcasted_iota(jnp.int32, (FRAG, 128), 1)
    total = jnp.zeros((FRAG, 128), jnp.float32)
    for b in range(FRAG):
        part = jnp.sum(jnp.sum(products[b], axis=1), axis=1, keepdims=True)
        total = total + jnp.where(lane == b, part, 0.0)
    block[...] = total
    sums = []
    for step, other in peers():
        sums.append(pltpu.make_async_remote_copy(
            src_ref=block, dst_ref=blocks.at[step], send_sem=send_sum.at[step], recv_sem=recv_sum.at[step],
            device_id={"grp": other}, device_id_type=MESH))
        sums[-1].start()
    for c in range(CHUNKS):
        for copy in slabs[c] + [ahead[c], back[c], on[c]] + [k for w in range(2) for k in picks[w][c] + sends[w][c]]:
            copy.wait_send()

        @pl.when(even)
        def _():
            side[c][0].wait_send()

        @pl.when(jnp.logical_not(even))
        def _():
            side[c][1].wait_send()

    for copy in sums + phi_outs + action_outs:
        copy.wait()
    total_ref[...] = ((block[...] + blocks[2]) + (blocks[1] + blocks[3])) / float(B**3)


def exchange(orbitals, kernel, anchors, count, first, second, reach):
    left, inverse, right, twiddle = (jnp.asarray(t) for t in tables())
    vmem, hbm = pl.BlockSpec(memory_space=pltpu.VMEM), pl.BlockSpec(memory_space=pltpu.HBM)
    dma, f32, bf16 = pltpu.SemaphoreType.DMA, jnp.float32, jnp.bfloat16
    per_chunk, per_peer = dma((CHUNKS,)), dma((CHUNKS, GRP))
    part = [pltpu.VMEM((FRAG, rows, 128), f32) for rows in PARTS]
    pick = [pltpu.VMEM((GRP, TURNS, rows, 128), f32) for rows in PARTS]
    return pl.pallas_call(
        exchange_kernel,
        out_shape=(jax.ShapeDtypeStruct((12 * FRAG, B * B), f32),
                   jax.ShapeDtypeStruct((12 * FRAG, B * B), f32),
                   jax.ShapeDtypeStruct((FRAG, 128), f32)),
        in_specs=[hbm] * 11,
        out_specs=(hbm, hbm, vmem),
        scratch_shapes=[p for p in part for _ in range(3)]
        + [p for p in pick for _ in range(2)]
        + pick * 2 + part * 4
        + [pltpu.VMEM(a.shape, a.dtype) for a in (orbitals, kernel, left, inverse, right, twiddle)]
        + [pltpu.SMEM(a.shape, a.dtype) for a in (anchors, count, first, second, reach)]
        + [pltpu.SMEM((4, FRAG * GRP * TURNS), f32)]
        + [pltpu.VMEM((2, ROWS, 128), f32),
           pltpu.VMEM((TURNS, 2, ROWS, 128), f32),
           pltpu.VMEM((TURNS, 2, ROWS, 128), f32),
           pltpu.VMEM((CH, 384), f32),
           pltpu.VMEM((288, 384), f32),
           pltpu.VMEM((288, 384), f32),
           pltpu.VMEM((2 * CH, 864), bf16),
           pltpu.VMEM((288, 912), bf16),
           pltpu.VMEM((1152, 768), bf16),
           pltpu.VMEM((2, CH, 384), f32),
           pltpu.VMEM((TILES + 2 * PADT, B + 2 * PADX, 128), f32),
           pltpu.VMEM((TURNS, TILES, B, 128), f32),
           pltpu.VMEM((912, 768), bf16),
           pltpu.VMEM((2 * TURNS * CH, 1152), bf16),
           pltpu.VMEM((2 * TURNS * CH, 768), f32),
           pltpu.VMEM((2 * CH, 768), f32),
           pltpu.VMEM((FRAG, FRAG, 8, 128), f32),
           pltpu.VMEM((FRAG, 128), f32),
           pltpu.VMEM((GRP, FRAG, 128), f32),
           pltpu.VMEM((FRAG, SLAB, 128), f32),
           pltpu.VMEM((12 * FRAG, B * B), f32),
           pltpu.VMEM((12 * FRAG, B * B), f32),
           dma((11,)), per_peer, per_peer, per_chunk, per_chunk, per_chunk, per_chunk, per_chunk,
           dma((2, CHUNKS, GRP)), dma((2, CHUNKS, GRP)), dma((2, CHUNKS, GRP)), dma((2, CHUNKS, GRP)),
           dma((2, CHUNKS)),
           per_chunk, per_chunk, per_chunk, per_chunk, dma((GRP,)), dma((GRP,))],
        compiler_params=pltpu.CompilerParams(collective_id=0, has_side_effects=True, vmem_limit_bytes=67043328),
        name="exchange",
    )(orbitals, kernel, left, inverse, right, twiddle, anchors, count, first, second, reach)


def project_kernel(phi_hbm, action_hbm, total_hbm, gradient_hbm, lagrange_hbm, phi, action, gradient, total_ref, lagrange_ref,
                   load_sem, store_sem, small_sem):
    band = 12 * FRAG // BANDS

    def at(k):
        return pl.ds(band * k, band)

    loads = [[pltpu.make_async_copy(s.at[at(k)], d.at[at(k)], load_sem.at[i, k])
              for i, (s, d) in enumerate(((phi_hbm, phi), (action_hbm, action)))] for k in range(BANDS)]
    stores = [pltpu.make_async_copy(gradient.at[at(k)], gradient_hbm.at[at(k)], store_sem.at[k]) for k in range(BANDS)]
    small = pltpu.make_async_copy(total_hbm, total_ref, small_sem.at[0])
    symmetric = pltpu.make_async_copy(lagrange_ref, lagrange_hbm, small_sem.at[1])
    small.start()
    for pair in loads:
        for load in pair:
            load.start()
    small.wait()
    total = total_ref[...][:, 0:FRAG]
    lagrange = 0.5 * (total + total.T)
    lagrange_ref[0] = lagrange
    symmetric.start()
    for k in range(BANDS):
        for load in loads[k]:
            load.wait()
        for x in range(band * k // FRAG, band * (k + 1) // FRAG):
            rows = slice(FRAG * x, FRAG * x + FRAG)
            value = action[rows, :]
            for b in range(FRAG):
                value = value - lagrange[:, b:b + 1] * phi[FRAG * x + b:FRAG * x + b + 1, :]
            gradient[rows, :] = value
        stores[k].start()
    for store in stores + [symmetric]:
        store.wait()


def projected(phi, action, total):
    hbm, dma = pl.BlockSpec(memory_space=pltpu.HBM), pltpu.SemaphoreType.DMA
    return pl.pallas_call(
        project_kernel,
        out_shape=(jax.ShapeDtypeStruct((12 * FRAG, B * B), jnp.float32),
                   jax.ShapeDtypeStruct((1, FRAG, FRAG), jnp.float32)),
        in_specs=[hbm] * 3,
        out_specs=(hbm, hbm),
        scratch_shapes=[pltpu.VMEM((12 * FRAG, B * B), jnp.float32)] * 3
        + [pltpu.VMEM((FRAG, 128), jnp.float32), pltpu.VMEM((1, FRAG, FRAG), jnp.float32),
           dma((2, BANDS)), dma((BANDS,)), dma((2,))],
        compiler_params=pltpu.CompilerParams(vmem_limit_bytes=67043328),
        name="projected",
    )(phi, action, total)


def shards(orbitals, kernel, anchors, pair_count, pair_first, pair_second, pair_reach):
    phi, action, total = exchange(orbitals, kernel, anchors.T, pair_count, pair_first, pair_second, pair_reach)
    gradient, lagrange = projected(phi, action, total)
    return gradient.reshape(12, FRAG, B * B).transpose(1, 0, 2), lagrange


def solution(mesh):
    placed = (P(("orb", "grp"), None, None), P(), P(), P("orb"), P("orb"), P("orb"), P("orb"))
    return jax.shard_map(
        shards,
        mesh=mesh,
        in_specs=placed,
        out_specs=(P("orb", "grp", None), P("orb", None, None)),
        check_vma=False,
    )
```
